128 devices in a mesh: ha: 16 (over x, z_hi, core), wa: 8 (over y, z_lo).
Axes of the slice: x: 4, y: 4, z: 4 (z_hi: 2, z_lo: 2; z = z_hi * 2 + z_lo), core: 2. Of those that a mesh axis runs over, the one named last changes fastest.
Arguments:
- frames: bfloat16 [2, 256, 512, 384], P(None, 'ha', 'wa'), may hold values from -6 to 6
- keep: int32 [2, 3], replicated, may hold values 0 or 1
- expand_weight: bfloat16 [384, 1536], replicated, may hold values from -0.3125 to 0.3125
- dw_kernel: float32 [3, 3, 1536], replicated, may hold values from -2 to 2
- conv_bias: float32 [1536], replicated, may hold values from -3 to 3
- project_weight: bfloat16 [1536, 384], replicated, may hold values from -0.15625 to 0.15625
- qkv_weight: bfloat16 [384, 1152], replicated, may hold values from -4 to 4
- out_weight: bfloat16 [384, 384], replicated, may hold values from -0.3125 to 0.3125
- mlp_in: bfloat16 [384, 1536], replicated, may hold values from -0.3125 to 0.3125
- mlp_out: bfloat16 [1536, 384], replicated, may hold values from -0.15625 to 0.15625
Outputs:
- result: bfloat16 [2, 256, 512, 384], P(None, 'ha', 'wa')
The draws below stay inside these ranges and needn't reach their ends.
All inputs are finite; a program needn't handle non-finite values.
Results may differ from the reference program's by a relative error of at most 0.0068.
Values may be sent and summed in bfloat16 or wider, within the bound.
A program may use at most 64 MiB of HBM per device.

```python
import math
import jax
import jax.numpy as jnp
from jax import lax

C = 384
EXP = 1536
HEADS = 12
FFN = 1536
GRID = 16
FRAMES = 2
H = 256
W = 512


def draw_qkv_weight(key, part):
    first_key = jax.random.fold_in(key, 0)
    whole = jax.random.normal(first_key, (C, 3 * C), jnp.float32) / math.sqrt(C)
    return jnp.clip(whole, -4.0, 4.0).astype(jnp.bfloat16)


def place_ends(array, stream_key, smallest, top_value):
    extent = array.shape
    spot = [jax.random.randint(jax.random.fold_in(stream_key, axis), (), 0, extent[axis]) for axis in range(len(extent))]
    array = array.at[tuple(spot)].set(smallest)
    longest = extent.index(max(extent))
    spot[longest] = (spot[longest] + 1) % extent[longest]
    return array.at[tuple(spot)].set(top_value)


def levels(stream_key, dims, shards, smallest, high):
    def one(axis_at, shards_of):
        draws = jax.random.uniform(jax.random.fold_in(jax.random.fold_in(stream_key, 6), axis_at), (shards_of,), jnp.float32, smallest / len(shards), high / len(shards))
        return jnp.repeat(jnp.exp(draws), dims[axis_at] // shards_of).reshape((-1,) + (1,) * (len(dims) - axis_at - 1))

    loudness = one(*shards[0])
    for cut in shards[1:]:
        loudness = loudness * one(*cut)
    return loudness


def normal_values(stream_key, extent, scale, limit, shards=(), kind=jnp.bfloat16):
    array = jax.random.normal(stream_key, extent, jnp.float32) * scale
    if len(shards) > 0:
        array = levels(stream_key, extent, shards, -0.22, 0.18) * array
    return jnp.clip(array, min=-limit, max=limit).astype(kind)


def setup_inputs(seed: int = 0) -> dict:
    key_of = jax.random.split(jax.random.key(seed), 11)
    return {
        "frames": normal_values(key_of[0], (FRAMES, H, W, C), 1.0, 6.0, ((1, 16), (2, 8))),
        "keep": place_ends((jax.random.randint(key_of[1], (FRAMES, 3), 0, 5) < 4).astype(jnp.int32), jax.random.fold_in(key_of[1], 1), 0, 1),
        "expand_weight": normal_values(key_of[2], (C, EXP), C ** -0.5, 0.3125),
        "dw_kernel": normal_values(key_of[3], (3, 3, EXP), 0.33, 2.0, (), jnp.float32),
        "conv_bias": normal_values(key_of[4], (EXP,), 0.5, 3.0, (), jnp.float32),
        "project_weight": normal_values(key_of[5], (EXP, C), EXP ** -0.5, 0.15625),
        "qkv_weight": draw_qkv_weight(jax.random.fold_in(key_of[10], 71), 0),
        "out_weight": normal_values(key_of[7], (C, C), C ** -0.5, 0.3125),
        "mlp_in": normal_values(key_of[8], (C, FFN), C ** -0.5, 0.3125),
        "mlp_out": normal_values(key_of[9], (FFN, C), FFN ** -0.5, 0.15625),
    }


def normalize(values):
    mean_val = lax.optimization_barrier(jnp.mean(values, axis=-1, keepdims=True))
    centred = values - mean_val
    variance = lax.optimization_barrier(jnp.mean(centred * centred, axis=-1, keepdims=True))
    return centred * lax.rsqrt(variance + 1e-05)

def conv_branch(padded_in, dw_kernel, conv_bias, expand_weight, project_weight):
    row_count = padded_in.shape[0] - 2
    col_count = padded_in.shape[1] - 2
    expanded = jax.nn.gelu(jnp.dot(padded_in, expand_weight, preferred_element_type=jnp.float32)).astype(jnp.bfloat16)
    total = jnp.zeros((row_count, col_count, expanded.shape[-1]), jnp.float32)
    for shift_y in range(3):
        for shift_x in range(3):
            total = total + expanded[shift_y:shift_y + row_count, shift_x:shift_x + col_count].astype(jnp.float32) * dw_kernel[shift_y, shift_x]
    mixed = jax.nn.gelu(total + conv_bias).astype(jnp.bfloat16)
    return jnp.dot(mixed, project_weight, preferred_element_type=jnp.float32)

def attend(block, window_flag, qkv_weight, out_weight):
    pair_count, token_count, channels = block.shape
    head_dim = channels // HEADS
    residual = block.astype(jnp.float32)
    normed = normalize(residual).astype(jnp.bfloat16)
    qkv = jnp.dot(normed, qkv_weight, preferred_element_type=jnp.float32).astype(jnp.bfloat16)
    queries = qkv[..., :channels].reshape(pair_count, token_count, HEADS, head_dim).astype(jnp.float32)
    keys_part = qkv[..., channels:2 * channels].reshape(pair_count, token_count, HEADS, head_dim).astype(jnp.float32)
    values_part = qkv[..., 2 * channels:].reshape(pair_count, token_count, HEADS, head_dim).astype(jnp.float32)
    scores = jnp.einsum('bqhd,bkhd->bhqk', queries, keys_part) * head_dim ** (-0.5)
    top_score = lax.optimization_barrier(jnp.max(scores, axis=-1, keepdims=True))
    weights = jnp.exp(scores - top_score)
    probs = (weights / lax.optimization_barrier(jnp.sum(weights, axis=-1, keepdims=True))).astype(jnp.bfloat16)
    attended = jnp.einsum('bhqk,bkhd->bqhd', probs.astype(jnp.float32), values_part)
    attended = attended.astype(jnp.bfloat16).reshape(pair_count, token_count, channels)
    update = jnp.dot(attended, out_weight, preferred_element_type=jnp.float32)
    return (residual + window_flag[:, None, None] * update).astype(jnp.bfloat16)

def mlp_piece(piece, flag, mlp_in, mlp_out):
    residual = piece.astype(jnp.float32)
    normed = normalize(residual).astype(jnp.bfloat16)
    inner = jax.nn.gelu(jnp.dot(normed, mlp_in, preferred_element_type=jnp.float32)).astype(jnp.bfloat16)
    return (residual + flag * jnp.dot(inner, mlp_out, preferred_element_type=jnp.float32)).astype(jnp.bfloat16)

def reference(frames, keep, expand_weight, dw_kernel, conv_bias, project_weight, qkv_weight, out_weight, mlp_in, mlp_out):
    flags = keep.astype(jnp.float32)
    block_rows = 16
    section_one = []
    for frame in range(FRAMES):
        padded = jnp.pad(frames[frame], ((1, 1), (1, 1), (0, 0)))

        def one_block(index):
            start = (index * block_rows).astype(jnp.int32)
            piece = lax.dynamic_slice_in_dim(padded, start, block_rows + 2, 0)
            return conv_branch(piece, dw_kernel, conv_bias, expand_weight, project_weight)
        branch = lax.map(one_block, jnp.arange(H // block_rows, dtype=jnp.int32)).reshape(H, W, C)
        section_one.append((frames[frame].astype(jnp.float32) + flags[frame, 0] * branch).astype(jnp.bfloat16))
    first = jnp.stack(section_one)
    windows = first.reshape(FRAMES, GRID, H // GRID, GRID, W // GRID, C).transpose(0, 2, 4, 1, 3, 5)
    windows = windows.reshape(-1, GRID * GRID, C)
    window_count = windows.shape[0]
    window_flags = jnp.repeat(flags[:, 1], window_count // FRAMES).reshape(window_count // 2, 2)
    blocks = windows.reshape(window_count // 2, 2, GRID * GRID, C)

    def one_pair(pair):
        return attend(pair[0], pair[1], qkv_weight, out_weight)
    second = lax.map(one_pair, (blocks, window_flags))
    second = second.reshape(FRAMES, H // GRID, W // GRID, GRID, GRID, C).transpose(0, 3, 1, 4, 2, 5).reshape(FRAMES, H, W, C)
    outputs = []
    for frame in range(FRAMES):
        pieces = second[frame].reshape(H // block_rows, block_rows, W, C)
        frame_flag = flags[frame, 2]

        def one_piece(piece):
            return mlp_piece(piece, frame_flag, mlp_in, mlp_out)
        outputs.append(lax.map(one_piece, pieces).reshape(H, W, C))
    return jnp.stack(outputs)
```

```python
import functools
import math

import jax
import jax.numpy as jnp
from jax import lax
from jax.experimental import pallas as pl
from jax.experimental.pallas import tpu as pltpu
from jax.sharding import PartitionSpec as P

MESH = pl.DeviceIdType.MESH
F32, BF16 = jnp.float32, jnp.bfloat16
HA, WA = 16, 8
DEV = HA * WA
FR, RO, CO, C, EX = 2, 16, 64, 384, 1536
HEADS, HD = 12, 32
CH = 256
GA, GB = math.sqrt(2 / math.pi), math.sqrt(2 / math.pi) * 0.044715


def gelu(v):
    half = 0.5 * v
    return half + half * jnp.tanh(v * (GA + GB * (v * v)))


def norm(v):
    c = v - jnp.mean(v, axis=-1, keepdims=True)
    return (c * lax.rsqrt(jnp.mean(c * c, axis=-1, keepdims=True) + 1e-05)).astype(BF16)


def put(ref, rows, value):
    for l in range(3):
        ref[l, rows, :] = value[:, 128 * l : 128 * l + 128]


def take(ref, rows):
    return jnp.concatenate([ref[l, rows, :] for l in range(3)], 1)


def dot(a, b):
    return jnp.dot(a, b, preferred_element_type=F32)


def kernel(
    x, keep, we, dwk, bias, wp, wqkv, wo, wi, w2, out,
    xp, cols, hb, e, kb, le, mx, s, r, z, o, t, fs,
    halo_send, halo_recv, s_send, s_recv, z_send, z_recv, entry,
):
    ha, wa = lax.axis_index("ha"), lax.axis_index("wa")
    me = ha * WA + wa
    own_x, own_g = ha // 4, lax.rem(ha, 4)

    def at(h, w):
        return {"ha": h, "wa": w}

    barrier = pltpu.get_barrier_semaphore()
    near = [(lax.rem(ha + i, HA), wa) for i in range(1, HA)]
    near += [(ha, lax.rem(wa + i, WA)) for i in range(1, WA)]
    for h, w in near:
        pl.semaphore_signal(barrier, 1, device_id=at(h, w), device_id_type=MESH)

    for k in range(9):
        kb[k] = jnp.broadcast_to(dwk[k : k + 1, :], (8, EX))
    kb[9] = jnp.broadcast_to(bias[...], (8, EX))

    def permute(f, _):
        put(t, slice(None), x[f].astype(F32).reshape(RO * CO, C))

        def one(row, _):
            for q in range(0, 8, 2):
                two = [take(t, pl.ds(row * CO + q + i, 8, stride=8)) for i in range(2)]
                xp[f, row, q * 8 : q * 8 + 16, :] = jnp.concatenate(two, 0).astype(BF16)
            return 0

        lax.fori_loop(0, RO, one, 0)
        for side in range(2):
            cols[side, f] = take(t, pl.ds(side * (CO - 1), RO, stride=CO)).astype(BF16)
        return 0

    lax.fori_loop(0, FR, permute, 0)

    pl.semaphore_wait(barrier, len(near))
    for h, w in near[HA - 1 :]:
        pl.semaphore_signal(entry, 1, device_id=at(h, w), device_id_type=MESH)

    def expand(f, _):
        def rows(q, _):
            tokens = xp[f, pl.ds(q * 4, 4)].reshape(256, C)
            for n in range(0, EX, CH):
                v = gelu(dot(tokens, we[:, n : n + CH]))
                e[f, pl.ds(q * 4 + 1, 4), 1:9, :, n : n + CH] = v.reshape(4, 8, 8, CH)
            return 0

        return lax.fori_loop(0, 4, rows, 0)

    expand(0, 0)
    pl.semaphore_wait(entry, WA - 1)

    up, down = lax.rem(ha + HA - 1, HA), lax.rem(ha + 1, HA)
    left, right = lax.rem(wa + WA - 1, WA), lax.rem(wa + 1, WA)

    def halo(f):
        moves = [
            (xp.at[f, RO - 1], hb.at[f, 0:64], (down, wa)),
            (xp.at[f, 0], hb.at[f, 64:128], (up, wa)),
        ]
        for side, w in ((1, right), (0, left)):
            for blk, h in ((0, down), (1, ha), (2, up)):
                first = 128 + (1 - side) * 48 + blk * 16
                moves.append((cols.at[side, f], hb.at[f, first : first + 16], (h, w)))
        return [
            pltpu.make_async_remote_copy(
                src, dst, halo_send.at[f, i], halo_recv.at[f, i], device_id=at(*to), device_id_type=MESH
            )
            for i, (src, dst, to) in enumerate(moves)
        ]

    halos = [halo(f) for f in range(FR)]
    for f in range(FR):
        for c in halos[f]:
            c.start()
    expand(1, 0)
    for f in range(FR):
        for c in halos[f]:
            c.wait()

    ok_up, ok_down = (ha > 0).astype(F32), (ha < HA - 1).astype(F32)
    ok_side = ((wa > 0).astype(F32), (wa < WA - 1).astype(F32))
    sub = lax.broadcasted_iota(jnp.int32, (8, EX), 0)

    def edges(f, _):
        tokens = hb[f]
        for n in range(0, EX, CH):
            v = gelu(dot(tokens, we[:, n : n + CH]))
            e[f, 0, 1:9, :, n : n + CH] = (v[0:64] * ok_up).reshape(8, 8, CH)
            e[f, RO + 1, 1:9, :, n : n + CH] = (v[64:128] * ok_down).reshape(8, 8, CH)
            for side in range(2):
                p = 128 + side * 48
                le[side, 0:16, n : n + CH] = v[p : p + 16] * (ok_side[side] * ok_up)
                le[side, 16:32, n : n + CH] = v[p + 16 : p + 32] * ok_side[side]
                le[side, 32:48, n : n + CH] = v[p + 32 : p + 48] * (ok_side[side] * ok_down)

        def fill(p, _):
            a = pltpu.roll(e[f, p, 8], 1, 0)
            e[f, p, 0] = jnp.where(sub == 0, jnp.broadcast_to(le[0, pl.ds(15 + p, 1), :], (8, EX)), a)
            b = pltpu.roll(e[f, p, 1], 7, 0)
            e[f, p, 9] = jnp.where(sub == 7, jnp.broadcast_to(le[1, pl.ds(15 + p, 1), :], (8, EX)), b)
            return 0

        lax.fori_loop(0, RO + 2, fill, 0)
        return 0

    lax.fori_loop(0, FR, edges, 0)

    def partner(i, g, k):
        h, w = lax.rem(own_x + i, 4) * 4 + g, lax.rem(wa + k, WA)
        return h, w

    def spread(src, dst, send, recv, f, g, gg):
        for i in range(4):
            for k in range(8):
                h, w = partner(i, g, k)
                copy = pltpu.make_async_remote_copy(
                    src.at[f, h * WA + w], dst.at[f, me], send.at[f], recv.at[f],
                    device_id=at(h, w), device_id_type=MESH,
                )
                if i == 0 and k == 0:

                    @pl.when(gg > 0)
                    def _():
                        copy.start()
                else:
                    copy.start()

    def arrived(src, dst, send, recv, f):
        return pltpu.make_async_remote_copy(
            src.at[f, 0 : DEV - 1], dst.at[f, 0 : DEV - 1], send.at[f], recv.at[f],
            device_id=at(ha, wa), device_id_type=MESH,
        )

    def conv(f, _):
        flag = keep[f, 0].astype(F32)

        def group(gg, _):
            g = lax.rem(own_g + gg, 4)

            def row(rr, _):
                y = g * 4 + rr
                for n in range(0, EX, 128):
                    acc = jnp.broadcast_to(kb[9, :, n : n + 128][None], (8, 8, 128))
                    for i in range(3):
                        for j in range(3):
                            acc = acc + e[f, y + i, j : j + 8, :, n : n + 128] * kb[3 * i + j, :, n : n + 128][None]
                    mx[pl.ds(rr * 64, 64), n : n + 128] = gelu(acc).reshape(64, 128).astype(BF16)
                return 0

            lax.fori_loop(0, 4, row, 0)
            tokens = xp[f, pl.ds(g * 4, 4)].reshape(256, C)
            put(fs, slice(None), tokens.astype(F32) + flag * dot(mx[...], wp[...]))
            for i in range(4):
                for k in range(8):
                    part = take(fs, pl.ds(i * 64 + (k % 2) * 32 + k // 2, 8, stride=4))
                    s[f, (i * 4 + g) * WA + k] = part.astype(BF16)
            spread(s, r, s_send, s_recv, f, g, gg)
            return 0

        lax.fori_loop(0, 4, group, 0)
        r[f, me] = s[f, me]
        return 0

    lax.fori_loop(0, FR, conv, 0)

    lane = lax.broadcasted_iota(jnp.int32, (256, 128), 1)
    ones = jnp.ones((256, 128), BF16)
    expo = HD**-0.5 * math.log2(math.e)

    def attention(f, _):
        arrived(s, r, s_send, s_recv, f).wait_recv()
        put(t, slice(None), r[f].astype(F32).reshape(DEV * 8, C))
        flag, flag_two = keep[f, 1].astype(F32), keep[f, 2].astype(F32)

        def window(j, _):
            first = jnp.concatenate([take(t, pl.ds(2 * j + h, DEV, stride=8)) for h in range(2)], 0)
            qkv = dot(norm(first), wqkv[...]).astype(BF16)
            parts = []
            for grp in range(3):
                q, k, v = (qkv[:, C * a + 128 * grp : C * a + 128 * grp + 128] for a in range(3))
                v = jnp.concatenate([v, ones], 1)
                att = None
                for h in range(4):
                    mine = (lane >= h * HD) & (lane < (h + 1) * HD)
                    qh = jnp.where(mine, q.astype(F32), 0.0).astype(BF16)
                    sc = lax.dot_general(qh, k, (((1,), (1,)), ((), ())), preferred_element_type=F32)
                    sc = sc - jnp.max(sc, axis=-1, keepdims=True)
                    pv = dot(jnp.exp2(sc * expo).astype(BF16), v)
                    pv = pv[:, :128] / pv[:, 128:]
                    att = pv if att is None else jnp.where(mine, pv, att)
                parts.append(att.astype(BF16))
            second = first + flag * dot(jnp.concatenate(parts, 1), wo[...])
            second = second.astype(BF16).astype(F32)
            for h in range(2):
                put(t, pl.ds(2 * j + h, DEV, stride=8), second[h * DEV : (h + 1) * DEV])
            return 0

        lax.fori_loop(0, 4, window, 0)

        def mlp(gg, _):
            g = lax.rem(own_g + gg, 4)
            second = jnp.concatenate([take(t, pl.ds((i * 4 + g) * 64, 64)) for i in range(4)], 0)
            normed = norm(second)
            for n in range(0, EX, CH):
                mx[:, n : n + CH] = gelu(dot(normed, wi[:, n : n + CH])).astype(BF16)
            res = (second + flag_two * dot(mx[...], w2[...])).astype(BF16)
            for i in range(4):
                z[f, pl.ds((i * 4 + g) * WA, WA)] = res[i * 64 : (i + 1) * 64].reshape(8, 8, C)
            spread(z, o, z_send, z_recv, f, g, gg)
            return 0

        lax.fori_loop(0, 4, mlp, 0)
        o[f, me] = z[f, me]
        return 0

    lax.fori_loop(0, FR, attention, 0)

    def gather(f, _):
        arrived(z, o, z_send, z_recv, f).wait_recv()

        def row(y, _):
            h = lax.rem(y, 4) * 4 + y // 4
            put(fs, slice(0, 64), o[f, pl.ds(h * WA, WA)].astype(F32).reshape(64, C))
            for half in range(2):
                out[f, y, half * 32 : half * 32 + 32] = take(fs, pl.ds(half, 32, stride=2)).astype(BF16)
            return 0

        lax.fori_loop(0, RO, row, 0)
        return 0

    lax.fori_loop(0, FR, gather, 0)
    for f in range(FR):
        arrived(s, r, s_send, s_recv, f).wait_send()
        arrived(z, o, z_send, z_recv, f).wait_send()


def body(frames, keep, we, dwk, bias, wp, wqkv, wo, wi, w2):
    vmem = pl.BlockSpec(memory_space=pltpu.VMEM)
    dma = pltpu.SemaphoreType.DMA
    slots = pltpu.VMEM((FR, DEV, 8, C), BF16)
    return pl.pallas_call(
        kernel,
        out_shape=jax.ShapeDtypeStruct(frames.shape, BF16),
        in_specs=[vmem, pl.BlockSpec(memory_space=pltpu.SMEM)] + [vmem] * 8,
        out_specs=vmem,
        scratch_shapes=[
            pltpu.VMEM((FR, RO, CO, C), BF16),
            pltpu.VMEM((2, FR, RO, C), BF16),
            pltpu.VMEM((FR, 224, C), BF16),
            pltpu.VMEM((FR, RO + 2, 10, 8, EX), F32),
            pltpu.VMEM((10, 8, EX), F32),
            pltpu.VMEM((2, 48, EX), F32),
            pltpu.VMEM((256, EX), BF16),
            slots, slots, slots, slots,
            pltpu.VMEM((3, DEV * 8, 128), F32),
            pltpu.VMEM((3, 256, 128), F32),
            dma((FR, 8)), dma((FR, 8)), dma((FR,)), dma((FR,)), dma((FR,)), dma((FR,)),
            pltpu.SemaphoreType.REGULAR,
        ],
        compiler_params=pltpu.CompilerParams(
            collective_id=0, has_side_effects=True, vmem_limit_bytes=60 * 1024 * 1024
        ),
        name="block",
    )(frames, keep, we, dwk.reshape(9, EX), bias.reshape(1, EX), wp, wqkv, wo, wi, w2)


def solution(mesh):
    in_specs = (P(None, "ha", "wa", None), P(), P(), P(), P(), P(), P(), P(), P(), P())
    return jax.shard_map(body, mesh=mesh, in_specs=in_specs, out_specs=P(None, "ha", "wa", None), check_vma=False)
```

```python
import functools
import math

import jax
import jax.numpy as jnp
from jax import lax
from jax.experimental import pallas as pl
from jax.experimental.pallas import tpu as pltpu
from jax.sharding import PartitionSpec as P

MESH = pl.DeviceIdType.MESH
F32, BF16 = jnp.float32, jnp.bfloat16
HA, WA = 16, 8
DEV = HA * WA
FR, RO, CO, C, EX = 2, 16, 64, 384, 1536
HEADS, HD = 12, 32
CH = 256
GA, GB = math.sqrt(2 / math.pi), math.sqrt(2 / math.pi) * 0.044715


def gelu(v):
    half = 0.5 * v
    return half + half * jnp.tanh(v * (GA + GB * (v * v)))


def norm(v):
    c = v - jnp.mean(v, axis=-1, keepdims=True)
    return (c * lax.rsqrt(jnp.mean(c * c, axis=-1, keepdims=True) + 1e-05)).astype(BF16)


def put(ref, rows, value):
    for l in range(3):
        ref[l, rows, :] = value[:, 128 * l : 128 * l + 128]


def take(ref, rows):
    return jnp.concatenate([ref[l, rows, :] for l in range(3)], 1)


def dot(a, b):
    return jnp.dot(a, b, preferred_element_type=F32)


def kernel(
    x_hbm, keep, we_hbm, dwk_hbm, bias_hbm, wp_hbm, wqkv_hbm, wo_hbm, wi_hbm, w2_hbm, out,
    x, we, dwk, bias, wp, wqkv, wo, wi, w2,
    xp, cols, hb, e, kb, le, mx, s, r, z, t, fs,
    loads, halo_send, halo_recv, s_send, s_recv, z_send, z_recv, own, entry,
):
    ha, wa = lax.axis_index("ha"), lax.axis_index("wa")
    me = ha * WA + wa
    own_x, own_g = ha // 4, lax.rem(ha, 4)

    def at(h, w):
        return {"ha": h, "wa": w}

    barrier = pltpu.get_barrier_semaphore()
    near = [(ha, lax.rem(wa + i, WA)) for i in range(1, WA)]
    near += [(lax.rem(ha + i, HA), wa) for i in range(1, HA)]
    near += [(lax.rem(ha + i, HA), lax.rem(wa + j, WA)) for i in (1, HA - 1) for j in (1, WA - 1)]
    for h, w in near:
        pl.semaphore_signal(barrier, 1, device_id=at(h, w), device_id_type=MESH)

    arrays = (
        (x_hbm, x), (we_hbm, we), (dwk_hbm, dwk), (bias_hbm, bias), (wp_hbm, wp),
        (wqkv_hbm, wqkv), (wo_hbm, wo), (wi_hbm, wi), (w2_hbm, w2),
    )
    fetch = [pltpu.make_async_copy(src, dst, loads.at[i]) for i, (src, dst) in enumerate(arrays)]
    for c in fetch:
        c.start()
    fetch[0].wait()

    def permute(f, _):
        put(t, slice(None), x[f].astype(F32).reshape(RO * CO, C))

        def one(row, _):
            for q in range(4):
                xp[f, row, q * 16 : q * 16 + 16, :] = take(t, pl.ds(row * CO + q, 16, stride=4)).astype(BF16)
            return 0

        lax.fori_loop(0, RO, one, 0)
        for side in range(2):
            cols[side, f] = take(t, pl.ds(side * (CO - 1), RO, stride=CO)).astype(BF16)
        return 0

    lax.fori_loop(0, FR, permute, 0)

    def expand(f, _):
        def rows(q, _):
            tokens = xp[f, pl.ds(q * 4, 4)].reshape(256, C)
            for n in range(0, EX, CH):
                v = gelu(dot(tokens, we[:, n : n + CH]).astype(BF16))
                e[f, pl.ds(q * 4 + 1, 4), 1:5, :, n : n + CH] = v.reshape(4, 4, 16, CH)
            return 0

        return lax.fori_loop(0, 4, rows, 0)

    pl.semaphore_wait(barrier, len(near))
    for h, w in near[: WA - 1]:
        pl.semaphore_signal(entry, 1, device_id=at(h, w), device_id_type=MESH)

    up, down = lax.rem(ha + HA - 1, HA), lax.rem(ha + 1, HA)
    left, right = lax.rem(wa + WA - 1, WA), lax.rem(wa + 1, WA)

    def halo(f):
        moves = [
            (xp.at[f, RO - 1], hb.at[f, 0:64], (down, wa)),
            (xp.at[f, 0], hb.at[f, 64:128], (up, wa)),
        ]
        for side, w in ((1, right), (0, left)):
            for blk, h in ((0, down), (1, ha), (2, up)):
                first = 128 + (1 - side) * 48 + blk * 16
                moves.append((cols.at[side, f], hb.at[f, first : first + 16], (h, w)))
        return [
            pltpu.make_async_remote_copy(
                src, dst, halo_send.at[f, i], halo_recv.at[f, i], device_id=at(*to), device_id_type=MESH
            )
            for i, (src, dst, to) in enumerate(moves)
        ]

    halos = [halo(f) for f in range(FR)]
    for f in range(FR):
        for c in halos[f]:
            c.start()
    fetch[1].wait()
    expand(0, 0)
    for c in fetch[2:]:
        c.wait()
    for i in range(3):
        for j in range(3):
            kb[3 * i + j] = jnp.broadcast_to(dwk[i, j : j + 1, :], (16, EX)).astype(BF16)
    kb[9] = jnp.broadcast_to(bias[...].reshape(1, EX), (16, EX)).astype(BF16)
    ok_up, ok_down = (ha > 0).astype(F32), (ha < HA - 1).astype(F32)
    ok_side = ((wa > 0).astype(F32), (wa < WA - 1).astype(F32))
    sub = lax.broadcasted_iota(jnp.int32, (16, EX), 0)

    def edges(f, _):
        tokens = hb[f]
        for n in range(0, EX, CH):
            v = gelu(dot(tokens, we[:, n : n + CH]))
            e[f, 0, 1:5, :, n : n + CH] = (v[0:64] * ok_up).astype(BF16).reshape(4, 16, CH)
            e[f, RO + 1, 1:5, :, n : n + CH] = (v[64:128] * ok_down).astype(BF16).reshape(4, 16, CH)
            for side in range(2):
                p = 128 + side * 48
                le[side, 0:16, n : n + CH] = v[p : p + 16] * (ok_side[side] * ok_up)
                le[side, 16:32, n : n + CH] = v[p + 16 : p + 32] * ok_side[side]
                le[side, 32:48, n : n + CH] = v[p + 32 : p + 48] * (ok_side[side] * ok_down)

        def fill(p, _):
            for side, (inner, outer, turn, edge) in enumerate(((4, 0, 1, 0), (1, 5, 15, 15))):
                moved = pltpu.roll(e[f, p, inner].astype(F32), turn, 0)
                beyond = jnp.broadcast_to(le[side, pl.ds(15 + p, 1), :], (16, EX))
                e[f, p, outer] = jnp.where(sub == edge, beyond, moved).astype(BF16)
            return 0

        lax.fori_loop(0, RO + 2, fill, 0)
        return 0


    def partner(i, g, k):
        h, w = lax.rem(own_x + i, 4) * 4 + g, lax.rem(wa + k, WA)
        return h, w

    def spread(src, dst, send, recv, f, gg, i):
        g = lax.rem(own_g + gg, 4)
        for k in range(8):
            if gg + i + k > 0:
                h, w = partner(i, g, k)
                pltpu.make_async_remote_copy(
                    src.at[f, h * WA + w], dst.at[f, me], send.at[f], recv.at[f],
                    device_id=at(h, w), device_id_type=MESH,
                ).start()

    def arrived(src, dst, send, recv, f):
        return pltpu.make_async_remote_copy(
            src.at[f, 0 : DEV - 1], dst.at[f, 0 : DEV - 1], send.at[f], recv.at[f],
            device_id=at(ha, wa), device_id_type=MESH,
        )

    pl.semaphore_wait(entry, WA - 1)

    def conv(f, _):
        flag = keep[f, 0].astype(F32)

        def row(gg, rr):
            y = lax.rem(own_g + gg, 4) * 4 + rr
            for n in range(0, EX, 128):
                sums = []
                for i in range(3):
                    taps = [e[f, y + i, j : j + 4, :, n : n + 128] * kb[3 * i + j, :, n : n + 128][None] for j in range(3)]
                    sums.append(taps[0] + taps[1] + taps[2])
                acc = (sums[0] + sums[1]) + (sums[2] + kb[9, :, n : n + 128][None])
                mx[gg % 2, rr * 64 : rr * 64 + 64, n : n + 128] = gelu(acc).reshape(64, 128)

        def project(gg):
            g = lax.rem(own_g + gg, 4)
            tokens = xp[f, pl.ds(g * 4, 4)].reshape(256, C)
            put(fs, slice(None), tokens.astype(F32) + flag * dot(mx[gg % 2], wp[...]))
            for i in range(4):
                for k in range(8):
                    part = take(fs, pl.ds(i * 64 + k, 8, stride=8))
                    s[f, (i * 4 + g) * WA + k] = part.astype(BF16)

        for gg in range(5):
            if gg > 0:
                project(gg - 1)
            for rr in range(4):
                if gg < 4:
                    row(gg, rr)
                if gg > 0:
                    spread(s, r, s_send, s_recv, f, gg - 1, rr)
        r[f, me] = s[f, me]
        return 0

    def front(f, _):
        @pl.when(f > 0)
        def _():
            expand(f, 0)

        for c in halo(f):
            c.wait()
        edges(f, 0)
        return conv(f, 0)

    lax.fori_loop(0, FR, front, 0)

    lane = lax.broadcasted_iota(jnp.int32, (256, 128), 1)
    heads = [(lane >= h * HD) & (lane < (h + 1) * HD) for h in range(4)]
    masks = [m.astype(F32).astype(BF16) for m in heads]
    ones = jnp.ones((256, 128), BF16)
    expo = HD**-0.5 * math.log2(math.e)

    def attention(f, _):
        arrived(s, r, s_send, s_recv, f).wait_recv()
        put(t, slice(None), r[f].astype(F32).reshape(DEV * 8, C))
        flag, flag_two = keep[f, 1].astype(F32), keep[f, 2].astype(F32)

        def window(j, _):
            first = jnp.concatenate([take(t, pl.ds(2 * j + h, DEV, stride=8)) for h in range(2)], 0)
            qkv = dot(norm(first), wqkv[...]).astype(BF16)
            parts = []
            for grp in range(3):
                q, k, v = (qkv[:, C * a + 128 * grp : C * a + 128 * grp + 128] for a in range(3))
                v = jnp.concatenate([v, ones], 1)
                att = None
                for h in range(4):
                    sc = lax.dot_general(q * masks[h], k, (((1,), (1,)), ((), ())), preferred_element_type=F32)
                    sc = sc - jnp.max(sc, axis=-1, keepdims=True)
                    pv = dot(jnp.exp2(sc * expo).astype(BF16), v)
                    pv = pv[:, :128] / pv[:, 128:]
                    att = pv if att is None else jnp.where(heads[h], pv, att)
                parts.append(att.astype(BF16))
            second = first + flag * dot(jnp.concatenate(parts, 1), wo[...])
            second = second.astype(BF16).astype(F32)
            for h in range(2):
                put(t, pl.ds(2 * j + h, DEV, stride=8), second[h * DEV : (h + 1) * DEV])
            return 0

        lax.fori_loop(0, 4, window, 0)

        def mlp(gg):
            g = lax.rem(own_g + gg, 4)
            second = jnp.concatenate([take(t, pl.ds((i * 4 + g) * 64, 64)) for i in range(4)], 0)
            normed = norm(second)
            for n in range(0, EX, CH):
                mx[gg % 2, :, n : n + CH] = gelu(dot(normed, wi[:, n : n + CH]).astype(BF16))
            res = (second + flag_two * dot(mx[gg % 2], w2[...])).astype(BF16)
            for i in range(4):
                z[f, pl.ds((i * 4 + g) * WA, WA)] = res[i * 64 : (i + 1) * 64].reshape(8, 8, C)

        for gg in range(5):
            if gg > 0:
                for i in range(4):
                    spread(z, out, z_send, z_recv, f, gg - 1, i)
            if gg < 4:
                mlp(gg)
        pltpu.make_async_copy(z.at[f, me], out.at[f, me], own.at[f]).start()
        return 0

    lax.fori_loop(0, FR, attention, 0)

    for f in range(FR):
        pltpu.make_async_copy(z.at[f, me], out.at[f, me], own.at[f]).wait()
        arrived(z, out, z_send, z_recv, f).wait_recv()
    for f in range(FR):
        arrived(s, r, s_send, s_recv, f).wait_send()
        arrived(z, out, z_send, z_recv, f).wait_send()


def gather(o, out, fs):
    for g in range(o.shape[2]):
        for i in range(4):
            n = 4 * g + i
            put(fs, slice(64 * n, 64 * n + 64), o[0, i, g].astype(F32).reshape(64, C))
            for half in range(2):
                part = take(fs, pl.ds(64 * n + half, 32, stride=2))
                out[0, n, half * 32 : half * 32 + 32] = part.astype(BF16)


def body(frames, keep, we, dwk, bias, wp, wqkv, wo, wi, w2):
    hbm = pl.BlockSpec(memory_space=pl.ANY)
    dma = pltpu.SemaphoreType.DMA
    slots = pltpu.VMEM((FR, DEV, 8, C), BF16)
    arrays = (frames, we, dwk, bias, wp, wqkv, wo, wi, w2)
    result = pl.pallas_call(
        kernel,
        out_shape=jax.ShapeDtypeStruct((FR, DEV, 8, C), BF16),
        in_specs=[hbm, pl.BlockSpec(memory_space=pltpu.SMEM)] + [hbm] * 8,
        out_specs=hbm,
        scratch_shapes=[pltpu.VMEM(a.shape, a.dtype) for a in arrays] + [
            pltpu.VMEM((FR, RO, CO, C), BF16),
            pltpu.VMEM((2, FR, RO, C), BF16),
            pltpu.VMEM((FR, 224, C), BF16),
            pltpu.VMEM((FR, RO + 2, 6, 16, EX), BF16),
            pltpu.VMEM((10, 16, EX), BF16),
            pltpu.VMEM((2, 48, EX), F32),
            pltpu.VMEM((2, 256, EX), BF16),
            slots, slots, slots,
            pltpu.VMEM((3, DEV * 8, 128), F32),
            pltpu.VMEM((3, 256, 128), F32),
            dma((len(arrays),)), dma((FR, 8)), dma((FR, 8)),
            dma((FR,)), dma((FR,)), dma((FR,)), dma((FR,)), dma((FR,)),
            pltpu.SemaphoreType.REGULAR,
        ],
        compiler_params=pltpu.CompilerParams(
            collective_id=0, has_side_effects=True, vmem_limit_bytes=60 * 1024 * 1024
        ),
        name="block",
    )(frames, keep, we, dwk, bias, wp, wqkv, wo, wi, w2)
    steps = 2
    return pl.pallas_call(
        gather,
        out_shape=jax.ShapeDtypeStruct(frames.shape, BF16),
        grid=(FR, steps),
        in_specs=[pl.BlockSpec((1, 4, 4 // steps, 8, 8, C), lambda f, g: (f, 0, g, 0, 0, 0))],
        out_specs=pl.BlockSpec((1, RO // steps, CO, C), lambda f, g: (f, g, 0, 0)),
        scratch_shapes=[pltpu.VMEM((3, RO // steps * CO, 128), F32)],
        name="rows",
    )(result.reshape(FR, 4, 4, 8, 8, C))


def solution(mesh):
    in_specs = (P(None, "ha", "wa", None), P(), P(), P(), P(), P(), P(), P(), P(), P())
    return jax.shard_map(body, mesh=mesh, in_specs=in_specs, out_specs=P(None, "ha", "wa", None), check_vma=False)
```

```python
import functools
import math

import jax
import jax.numpy as jnp
from jax import lax
from jax.experimental import pallas as pl
from jax.experimental.pallas import tpu as pltpu
from jax.sharding import PartitionSpec as P

MESH = pl.DeviceIdType.MESH
F32, BF16 = jnp.float32, jnp.bfloat16
HA, WA = 16, 8
DEV = HA * WA
FR, RO, CO, C, EX = 2, 16, 64, 384, 1536
HEADS, HD = 12, 32
UNROLL = 2
CH = 256
GA, GB = math.sqrt(2 / math.pi), math.sqrt(2 / math.pi) * 0.044715


def gelu(v):
    half = 0.5 * v
    return half + half * jnp.tanh(v * (GA + GB * (v * v)))


def gelu_of_half(half):
    return half + half * jnp.tanh(half * (2 * GA + 8 * GB * (half * half)))


def norm(v):
    c = v - jnp.mean(v, axis=-1, keepdims=True)
    return (c * lax.rsqrt(jnp.mean(c * c, axis=-1, keepdims=True) + 1e-05)).astype(BF16)


def put(ref, rows, value):
    for l in range(3):
        ref[l, rows, :] = value[:, 128 * l : 128 * l + 128]


def take(ref, rows):
    return jnp.concatenate([ref[l, rows, :] for l in range(3)], 1)


def dot(a, b):
    return jnp.dot(a, b, preferred_element_type=F32)


def kernel(
    x_hbm, keep, we_hbm, dwk_hbm, bias_hbm, wp_hbm, wqkv_hbm, wo_hbm, wi_hbm, w2_hbm, out,
    x, we, dwk, bias, wp, wqkv, wo, wi, w2,
    xp, cols, hb, e, kb, le, mx, s, r, z, o, t, fs,
    loads, halo_send, halo_recv, s_send, s_recv, z_send, z_recv, own, entry,
):
    ha, wa = lax.axis_index("ha"), lax.axis_index("wa")
    me = ha * WA + wa
    own_x, own_g = ha // 4, lax.rem(ha, 4)

    def at(h, w):
        return {"ha": h, "wa": w}

    barrier = pltpu.get_barrier_semaphore()
    near = [(ha, lax.rem(wa + i, WA)) for i in range(1, WA)]
    near += [(lax.rem(ha + i, HA), wa) for i in range(1, HA)]
    near += [(lax.rem(ha + i, HA), lax.rem(wa + j, WA)) for i in (1, HA - 1) for j in (1, WA - 1)]
    for h, w in near:
        pl.semaphore_signal(barrier, 1, device_id=at(h, w), device_id_type=MESH)

    arrays = (
        (x_hbm, x), (we_hbm, we), (dwk_hbm, dwk), (bias_hbm, bias), (wp_hbm, wp),
        (wqkv_hbm, wqkv), (wo_hbm, wo), (wi_hbm, wi), (w2_hbm, w2),
    )
    fetch = [pltpu.make_async_copy(src, dst, loads.at[i]) for i, (src, dst) in enumerate(arrays)]
    for c in fetch:
        c.start()
    fetch[0].wait()

    def permute(f, _):
        put(t, slice(None), x[f].astype(F32).reshape(RO * CO, C))

        def one(row, _):
            for q in range(4):
                xp[f, row, q * 16 : q * 16 + 16, :] = take(t, pl.ds(row * CO + q, 16, stride=4)).astype(BF16)
            return 0

        lax.fori_loop(0, RO, one, 0)
        for side in range(2):
            cols[side, f] = take(t, pl.ds(side * (CO - 1), RO, stride=CO)).astype(BF16)
        return 0

    lax.fori_loop(0, FR, permute, 0)

    def expand(f, _):
        def rows(q, _):
            tokens = xp[f, pl.ds(q * 4, 4)].reshape(256, C)
            for n in range(0, EX, CH):
                v = gelu(dot(tokens, we[:, n : n + CH]).astype(BF16))
                e[f, pl.ds(q * 4 + 1, 4), 1:5, :, n : n + CH] = v.reshape(4, 4, 16, CH)
            return 0

        return lax.fori_loop(0, 4, rows, 0)

    pl.semaphore_wait(barrier, len(near))
    for h, w in near[: WA - 1]:
        pl.semaphore_signal(entry, 1, device_id=at(h, w), device_id_type=MESH)

    up, down = lax.rem(ha + HA - 1, HA), lax.rem(ha + 1, HA)
    left, right = lax.rem(wa + WA - 1, WA), lax.rem(wa + 1, WA)

    def halo(f):
        moves = [
            (xp.at[f, RO - 1], hb.at[f, 0:64], (down, wa)),
            (xp.at[f, 0], hb.at[f, 64:128], (up, wa)),
        ]
        for side, w in ((1, right), (0, left)):
            for blk, h in ((0, down), (1, ha), (2, up)):
                first = 128 + (1 - side) * 48 + blk * 16
                moves.append((cols.at[side, f], hb.at[f, first : first + 16], (h, w)))
        return [
            pltpu.make_async_remote_copy(
                src, dst, halo_send.at[f, i], halo_recv.at[f, i], device_id=at(*to), device_id_type=MESH
            )
            for i, (src, dst, to) in enumerate(moves)
        ]

    halos = [halo(f) for f in range(FR)]
    for f in range(FR):
        for c in halos[f]:
            c.start()
    fetch[1].wait()
    expand(0, 0)
    for c in fetch[2:]:
        c.wait()
    for i in range(3):
        for j in range(3):
            kb[3 * i + j] = jnp.broadcast_to(0.5 * dwk[i, j : j + 1, :], (16, EX))
    kb[9] = jnp.broadcast_to(0.5 * bias[...].reshape(1, EX), (16, EX))
    ok_up, ok_down = (ha > 0).astype(F32), (ha < HA - 1).astype(F32)
    ok_side = ((wa > 0).astype(F32), (wa < WA - 1).astype(F32))
    sub = lax.broadcasted_iota(jnp.int32, (16, EX), 0)

    def edges(f, _):
        tokens = hb[f]
        for n in range(0, EX, CH):
            v = gelu(dot(tokens, we[:, n : n + CH]).astype(BF16))
            e[f, 0, 1:5, :, n : n + CH] = (v[0:64] * ok_up.astype(BF16)).reshape(4, 16, CH)
            e[f, RO + 1, 1:5, :, n : n + CH] = (v[64:128] * ok_down.astype(BF16)).reshape(4, 16, CH)
            v = v[128:].astype(F32)
            for side in range(2):
                p = side * 48
                le[side, 0:16, n : n + CH] = v[p : p + 16] * (ok_side[side] * ok_up)
                le[side, 16:32, n : n + CH] = v[p + 16 : p + 32] * ok_side[side]
                le[side, 32:48, n : n + CH] = v[p + 32 : p + 48] * (ok_side[side] * ok_down)

        def fill(p, _):
            for side, (inner, outer, turn, edge) in enumerate(((4, 0, 1, 0), (1, 5, 15, 15))):
                moved = pltpu.roll(e[f, p, inner].astype(F32), turn, 0)
                beyond = jnp.broadcast_to(le[side, pl.ds(15 + p, 1), :], (16, EX))
                e[f, p, outer] = jnp.where(sub == edge, beyond, moved).astype(BF16)
            return 0

        lax.fori_loop(0, RO + 2, fill, 0)
        return 0


    def partner(i, g, k):
        h, w = lax.rem(own_x + i, 4) * 4 + g, lax.rem(wa + k, WA)
        return h, w

    def spread(src, dst, send, recv, gg):
        g = lax.rem(own_g + gg, 4)
        for i in range(4):
            for k in range(8):
                h, w = partner(i, g, k)
                copy = pltpu.make_async_remote_copy(
                    src.at[h * WA + w], dst.at[me], send, recv, device_id=at(h, w), device_id_type=MESH
                )
                if i + k > 0:
                    copy.start()
                else:
                    pl.when(gg > 0)(copy.start)

    def arrived(src, dst, send, recv):
        return pltpu.make_async_remote_copy(
            src.at[0 : DEV - 1], dst.at[0 : DEV - 1], send, recv, device_id=at(ha, wa), device_id_type=MESH
        )

    pl.semaphore_wait(entry, WA - 1)

    def conv(f, _):
        flag = keep[f, 0].astype(F32)

        def group(gg, _):
            g = lax.rem(own_g + gg, 4)
            for rr in range(0, 4, 2):
                for n in range(0, EX, 128):
                    taps = [kb[i, :, n : n + 128].astype(BF16)[None] for i in range(10)]
                    for q in range(rr, rr + 2):
                        sums = []
                        for i in range(3):
                            part = [taps[3 * i + j] * e[f, g * 4 + q + i, j : j + 4, :, n : n + 128] for j in range(3)]
                            sums.append(part[0] + part[1] + part[2])
                        acc = (sums[0] + sums[1]) + (sums[2] + taps[9])
                        mx[q * 64 : q * 64 + 64, n : n + 128] = gelu_of_half(acc).reshape(64, 128)
            tokens = xp[f, pl.ds(g * 4, 4)].reshape(256, C)
            put(fs, slice(None), tokens.astype(F32) + flag * dot(mx[...], wp[...]))
            for i in range(4):
                for k in range(8):
                    part = take(fs, pl.ds(i * 64 + k, 8, stride=8))
                    s[f, (i * 4 + g) * WA + k] = part.astype(BF16)
            spread(s.at[f], r.at[f], s_send.at[f], s_recv.at[f], gg)
            return 0

        lax.fori_loop(0, 4, group, 0)
        r[f, me] = s[f, me]
        return 0

    def front(f, _):
        @pl.when(f > 0)
        def _():
            expand(f, 0)

        for c in halo(f):
            c.wait()
        edges(f, 0)
        return conv(f, 0)

    lax.fori_loop(0, FR, front, 0)

    lane = lax.broadcasted_iota(jnp.int32, (256, 128), 1)
    heads = [(lane >= h * HD) & (lane < (h + 1) * HD) for h in range(4)]
    masks = [m.astype(F32).astype(BF16) for m in heads]
    ones = jnp.ones((256, 128), BF16)
    expo = HD**-0.5 * math.log2(math.e)

    def mlp(second, flag):
        normed = norm(second)
        for n in range(0, EX, CH):
            mx[:, n : n + CH] = gelu(dot(normed, wi[:, n : n + CH]).astype(BF16))
        return (second + flag * dot(mx[...], w2[...])).astype(BF16)

    def attention(f, _):
        arrived(s.at[f], r.at[f], s_send.at[f], s_recv.at[f]).wait_recv()
        put(t, slice(None), r[f].astype(F32).reshape(DEV * 8, C))
        flag = keep[f, 1].astype(F32)

        def window(j, _):
            first = jnp.concatenate([take(t, pl.ds(2 * j + h, DEV, stride=8)) for h in range(2)], 0)
            qkv = dot(norm(first), wqkv[...]).astype(BF16)
            parts = []
            for grp in range(3):
                q, k, v = (qkv[:, C * a + 128 * grp : C * a + 128 * grp + 128] for a in range(3))
                v = jnp.concatenate([v, ones], 1)
                att = None
                for h in range(4):
                    sc = lax.dot_general(q * masks[h], k, (((1,), (1,)), ((), ())), preferred_element_type=F32)
                    sc = sc - jnp.max(sc, axis=-1, keepdims=True)
                    pv = dot(jnp.exp2(sc * expo).astype(BF16), v)
                    pv = pv[:, :128] / pv[:, 128:]
                    att = pv if att is None else jnp.where(heads[h], pv, att)
                parts.append(att.astype(BF16))
            second = first + flag * dot(jnp.concatenate(parts, 1), wo[...])
            second = second.astype(BF16).astype(F32)
            for h in range(2):
                put(t, pl.ds(2 * j + h, DEV, stride=8), second[h * DEV : (h + 1) * DEV])
            return 0

        def windows(p, _):
            for u in range(UNROLL):
                window(p * UNROLL + u, 0)
            return 0

        lax.fori_loop(0, 4 // UNROLL, windows, 0)

        @pl.when(f == 0)
        def _():
            z[0] = take(t, slice(None)).astype(BF16).reshape(DEV, 8, C)

            def send(gg, _):
                spread(z.at[0], o, z_send.at[0], z_recv.at[0], gg)
                return 0

            lax.fori_loop(0, 4, send, 0)
            o[me] = z[0, me]

        @pl.when(f == 1)
        def _():
            def block(gg, _):
                g = lax.rem(own_g + gg, 4)
                second = jnp.concatenate([take(t, pl.ds((i * 4 + g) * 64, 64)) for i in range(4)], 0)
                res = mlp(second, keep[1, 2].astype(F32))
                for i in range(4):
                    z[1, pl.ds((i * 4 + g) * WA, WA)] = res[i * 64 : (i + 1) * 64].reshape(8, 8, C)
                spread(z.at[1], out.at[1], z_send.at[1], z_recv.at[1], gg)
                return 0

            lax.fori_loop(0, 4, block, 0)
            pltpu.make_async_copy(z.at[1, me], out.at[1, me], own.at[1]).start()

        return 0

    lax.fori_loop(0, FR, attention, 0)
    arrived(z.at[0], o, z_send.at[0], z_recv.at[0]).wait_recv()

    def home(b, _):
        part = pl.ds(b * 32, 32)
        second = o[part].astype(F32).reshape(256, C)
        r[0, part] = mlp(second, keep[0, 2].astype(F32)).reshape(32, 8, C)
        pltpu.make_async_copy(r.at[0, part], out.at[0, part], own.at[0]).start()
        return 0

    lax.fori_loop(0, 4, home, 0)
    pltpu.make_async_copy(r.at[0], out.at[0], own.at[0]).wait()
    pltpu.make_async_copy(z.at[1, me], out.at[1, me], own.at[1]).wait()
    arrived(z.at[1], out.at[1], z_send.at[1], z_recv.at[1]).wait_recv()
    arrived(z.at[1], out.at[1], z_send.at[1], z_recv.at[1]).wait_send()
    arrived(z.at[0], o, z_send.at[0], z_recv.at[0]).wait_send()
    for f in range(FR):
        arrived(s.at[f], r.at[f], s_send.at[f], s_recv.at[f]).wait_send()


def gather(o, out, fs):
    for g in range(o.shape[2]):
        for i in range(4):
            n = 4 * g + i
            put(fs, slice(64 * n, 64 * n + 64), o[0, i, g].astype(F32).reshape(64, C))
            for half in range(2):
                part = take(fs, pl.ds(64 * n + half, 32, stride=2))
                out[0, n, half * 32 : half * 32 + 32] = part.astype(BF16)


def body(frames, keep, we, dwk, bias, wp, wqkv, wo, wi, w2):
    hbm = pl.BlockSpec(memory_space=pl.ANY)
    dma = pltpu.SemaphoreType.DMA
    slots = pltpu.VMEM((FR, DEV, 8, C), BF16)
    arrays = (frames, we, dwk, bias, wp, wqkv, wo, wi, w2)
    result = pl.pallas_call(
        kernel,
        out_shape=jax.ShapeDtypeStruct((FR, DEV, 8, C), BF16),
        in_specs=[hbm, pl.BlockSpec(memory_space=pltpu.SMEM)] + [hbm] * 8,
        out_specs=hbm,
        scratch_shapes=[pltpu.VMEM(a.shape, a.dtype) for a in arrays] + [
            pltpu.VMEM((FR, RO, CO, C), BF16),
            pltpu.VMEM((2, FR, RO, C), BF16),
            pltpu.VMEM((FR, 224, C), BF16),
            pltpu.VMEM((FR, RO + 2, 6, 16, EX), BF16),
            pltpu.VMEM((10, 16, EX), F32),
            pltpu.VMEM((2, 48, EX), F32),
            pltpu.VMEM((256, EX), BF16),
            slots, slots, slots,
            pltpu.VMEM((DEV, 8, C), BF16),
            pltpu.VMEM((3, DEV * 8, 128), F32),
            pltpu.VMEM((3, 256, 128), F32),
            dma((len(arrays),)), dma((FR, 8)), dma((FR, 8)),
            dma((FR,)), dma((FR,)), dma((FR,)), dma((FR,)), dma((FR,)),
            pltpu.SemaphoreType.REGULAR,
        ],
        compiler_params=pltpu.CompilerParams(
            collective_id=0, has_side_effects=True, vmem_limit_bytes=60 * 1024 * 1024
        ),
        name="block",
    )(frames, keep, we, dwk, bias, wp, wqkv, wo, wi, w2)
    steps = 2
    return pl.pallas_call(
        gather,
        out_shape=jax.ShapeDtypeStruct(frames.shape, BF16),
        grid=(FR, steps),
        in_specs=[pl.BlockSpec((1, 4, 4 // steps, 8, 8, C), lambda f, g: (f, 0, g, 0, 0, 0))],
        out_specs=pl.BlockSpec((1, RO // steps, CO, C), lambda f, g: (f, g, 0, 0)),
        scratch_shapes=[pltpu.VMEM((3, RO // steps * CO, 128), F32)],
        name="rows",
    )(result.reshape(FR, 4, 4, 8, 8, C))


def solution(mesh):
    in_specs = (P(None, "ha", "wa", None), P(), P(), P(), P(), P(), P(), P(), P(), P())
    return jax.shard_map(body, mesh=mesh, in_specs=in_specs, out_specs=P(None, "ha", "wa", None), check_vma=False)
```

```python
import functools
import math

import jax
import jax.numpy as jnp
from jax import lax
from jax.experimental import pallas as pl
from jax.experimental.pallas import tpu as pltpu
from jax.sharding import PartitionSpec as P

MESH = pl.DeviceIdType.MESH
F32, BF16 = jnp.float32, jnp.bfloat16
HA, WA = 16, 8
DEV = HA * WA
FR, RO, CO, C, EX = 2, 16, 64, 384, 1536
HEADS, HD = 12, 32
UNROLL = 2
CH = 256
GA, GB = math.sqrt(2 / math.pi), math.sqrt(2 / math.pi) * 0.044715


def gelu(v):
    half = 0.5 * v
    return half + half * jnp.tanh(v * (GA + GB * (v * v)))


def gelu_of_half(half):
    return half + half * jnp.tanh(half * (2 * GA + 8 * GB * (half * half)))


def norm(v):
    c = v - jnp.mean(v, axis=-1, keepdims=True)
    return (c * lax.rsqrt(jnp.mean(c * c, axis=-1, keepdims=True) + 1e-05)).astype(BF16)


def put(ref, rows, value):
    for l in range(3):
        ref[l, rows, :] = value[:, 128 * l : 128 * l + 128]


def take(ref, rows):
    return jnp.concatenate([ref[l, rows, :] for l in range(3)], 1)


def dot(a, b):
    return jnp.dot(a, b, preferred_element_type=F32)


def kernel(
    x_hbm, keep, we_hbm, dwk_hbm, bias_hbm, wp_hbm, wqkv_hbm, wo_hbm, wi_hbm, w2_hbm, out,
    x, we, dwk, bias, wp, wqkv, wo, wi, w2,
    xp, cols, hb, e_first, e_second, kb, le, mx, s, r, z, o, t, fs,
    loads, halo_send, halo_recv, s_send, s_recv, z_send, z_recv, own, entry,
):
    ha, wa = lax.axis_index("ha"), lax.axis_index("wa")
    me = ha * WA + wa
    own_x, own_g = ha // 4, lax.rem(ha, 4)
    e = (e_first, e_second)

    def at(h, w):
        return {"ha": h, "wa": w}

    barrier = pltpu.get_barrier_semaphore()
    near = [(ha, lax.rem(wa + i, WA)) for i in range(1, WA)]
    near += [(lax.rem(ha + i, HA), wa) for i in range(1, HA)]
    near += [(lax.rem(ha + i, HA), lax.rem(wa + j, WA)) for i in (1, HA - 1) for j in (1, WA - 1)]
    for h, w in near:
        pl.semaphore_signal(barrier, 1, device_id=at(h, w), device_id_type=MESH)

    arrays = (
        (x_hbm.at[0], x.at[0]), (x_hbm.at[1], x.at[1]), (we_hbm, we), (dwk_hbm, dwk), (bias_hbm, bias), (wp_hbm, wp),
        (wqkv_hbm, wqkv), (wo_hbm, wo), (wi_hbm, wi), (w2_hbm, w2),
    )
    fetch = [pltpu.make_async_copy(src, dst, loads.at[i]) for i, (src, dst) in enumerate(arrays)]
    for c in fetch:
        c.start()

    def permute(f):
        put(t, slice(None), x[f].astype(F32).reshape(RO * CO, C))

        def one(row, _):
            for q in range(4):
                xp[f, row, q * 16 : q * 16 + 16, :] = take(t, pl.ds(row * CO + q, 16, stride=4)).astype(BF16)
            return 0

        lax.fori_loop(0, RO, one, 0)
        for side in range(2):
            cols[side, f] = take(t, pl.ds(side * (CO - 1), RO, stride=CO)).astype(BF16)

    def expand(f, first, count):
        tokens = xp[f, pl.ds(first, count)].reshape(count * 64, C)
        for n in range(0, EX, CH):
            v = gelu(dot(tokens, we[:, n : n + CH]).astype(BF16))
            e[f][pl.ds(first + 1, count), 1:5, :, n : n + CH] = v.reshape(count, 4, 16, CH)

    up, down = lax.rem(ha + HA - 1, HA), lax.rem(ha + 1, HA)
    left, right = lax.rem(wa + WA - 1, WA), lax.rem(wa + 1, WA)

    def halo(f):
        moves = [
            (xp.at[f, RO - 1], hb.at[f, 0:64], (down, wa)),
            (xp.at[f, 0], hb.at[f, 64:128], (up, wa)),
        ]
        for side, w in ((1, right), (0, left)):
            for blk, h in ((0, down), (1, ha), (2, up)):
                first = 128 + (1 - side) * 48 + blk * 16
                moves.append((cols.at[side, f], hb.at[f, first : first + 16], (h, w)))
        return [
            pltpu.make_async_remote_copy(
                src, dst, halo_send.at[f, i], halo_recv.at[f, i], device_id=at(*to), device_id_type=MESH
            )
            for i, (src, dst, to) in enumerate(moves)
        ]

    for f in range(FR):
        fetch[f].wait()
        permute(f)
        if f == 0:
            pl.semaphore_wait(barrier, len(near))
            for h, w in near[: WA - 1]:
                pl.semaphore_signal(entry, 1, device_id=at(h, w), device_id_type=MESH)
        for c in halo(f):
            c.start()
    fetch[2].wait()
    for q in range(2):
        expand(0, q * 8, 8)
    for c in fetch[3:]:
        c.wait()
    for i in range(3):
        for j in range(3):
            kb[3 * i + j] = jnp.broadcast_to(0.5 * dwk[i, j : j + 1, :], (16, EX))
    kb[9] = jnp.broadcast_to(0.5 * bias[...].reshape(1, EX), (16, EX))
    ok_up, ok_down = (ha > 0).astype(F32), (ha < HA - 1).astype(F32)
    ok_side = ((wa > 0).astype(F32), (wa < WA - 1).astype(F32))
    sub = lax.broadcasted_iota(jnp.int32, (16, EX), 0)

    def edges(f):
        tokens = hb[f]
        for n in range(0, EX, CH):
            v = gelu(dot(tokens, we[:, n : n + CH]).astype(BF16))
            e[f][0, 1:5, :, n : n + CH] = (v[0:64] * ok_up.astype(BF16)).reshape(4, 16, CH)
            e[f][RO + 1, 1:5, :, n : n + CH] = (v[64:128] * ok_down.astype(BF16)).reshape(4, 16, CH)
            v = v[128:].astype(F32)
            for side in range(2):
                p = side * 48
                le[side, 0:16, n : n + CH] = v[p : p + 16] * (ok_side[side] * ok_up)
                le[side, 16:32, n : n + CH] = v[p + 16 : p + 32] * ok_side[side]
                le[side, 32:48, n : n + CH] = v[p + 32 : p + 48] * (ok_side[side] * ok_down)

        def fill(p, _):
            for side, (inner, outer, turn, edge) in enumerate(((4, 0, 1, 0), (1, 5, 15, 15))):
                moved = pltpu.roll(e[f][p, inner].astype(F32), turn, 0)
                beyond = jnp.broadcast_to(le[side, pl.ds(15 + p, 1), :], (16, EX))
                e[f][p, outer] = jnp.where(sub == edge, beyond, moved).astype(BF16)
            return 0

        lax.fori_loop(0, RO + 2, fill, 0)


    def partner(i, g, k):
        h, w = lax.rem(own_x + i, 4) * 4 + g, lax.rem(wa + k, WA)
        return h, w

    def spread(src, dst, send, recv, gg):
        g = lax.rem(own_g + gg, 4)
        for i in range(4):
            for k in range(8):
                h, w = partner(i, g, k)
                copy = pltpu.make_async_remote_copy(
                    src.at[h * WA + w], dst.at[me], send, recv, device_id=at(h, w), device_id_type=MESH
                )
                if i + k > 0:
                    copy.start()
                else:
                    pl.when(gg > 0)(copy.start)

    def arrived(src, dst, send, recv):
        return pltpu.make_async_remote_copy(
            src.at[0 : DEV - 1], dst.at[0 : DEV - 1], send, recv, device_id=at(ha, wa), device_id_type=MESH
        )

    pl.semaphore_wait(entry, WA - 1)

    def conv(f):
        flag = keep[f, 0].astype(F32)

        def group(gg, _):
            g = lax.rem(own_g + gg, 4)
            if f == 0:
                expand(1, gg * 4, 4)
            for rr in range(0, 4, 2):
                for n in range(0, EX, 128):
                    taps = [kb[i, :, n : n + 128].astype(BF16)[None] for i in range(10)]
                    for q in range(rr, rr + 2):
                        sums = []
                        for i in range(3):
                            part = [taps[3 * i + j] * e[f][g * 4 + q + i, j : j + 4, :, n : n + 128] for j in range(3)]
                            sums.append(part[0] + part[1] + part[2])
                        acc = (sums[0] + sums[1]) + (sums[2] + taps[9])
                        mx[q * 64 : q * 64 + 64, n : n + 128] = gelu_of_half(acc).reshape(64, 128)
            tokens = xp[f, pl.ds(g * 4, 4)].reshape(256, C)
            put(fs, slice(None), tokens.astype(F32) + flag * dot(mx[0:256], wp[...]))
            for i in range(4):
                for k in range(8):
                    part = take(fs, pl.ds(i * 64 + k, 8, stride=8))
                    s[f, (i * 4 + g) * WA + k] = part.astype(BF16)
            spread(s.at[f], r.at[f], s_send.at[f], s_recv.at[f], gg)
            return 0

        lax.fori_loop(0, 4, group, 0)
        r[f, me] = s[f, me]

    for f in range(FR):
        for c in halo(f):
            c.wait()
        edges(f)
        conv(f)

    lane = lax.broadcasted_iota(jnp.int32, (256, 128), 1)
    heads = [(lane >= h * HD) & (lane < (h + 1) * HD) for h in range(4)]
    masks = [m.astype(F32).astype(BF16) for m in heads]
    ones = jnp.ones((256, 128), BF16)
    expo = HD**-0.5 * math.log2(math.e)

    def mlp(second, flag):
        normed = norm(second)
        for n in range(0, EX, CH):
            mx[:, n : n + CH] = gelu(dot(normed, wi[:, n : n + CH]).astype(BF16))
        return (second + flag * dot(mx[...], w2[...])).astype(BF16)

    def attention(f, _):
        arrived(s.at[f], r.at[f], s_send.at[f], s_recv.at[f]).wait_recv()
        put(t, slice(None), r[f].astype(F32).reshape(DEV * 8, C))
        flag = keep[f, 1].astype(F32)

        def windows(p, _):
            rows = [pl.ds(2 * p * UNROLL + i, DEV, stride=8) for i in range(2 * UNROLL)]
            first = jnp.concatenate([take(t, part) for part in rows], 0)
            all_qkv = dot(norm(first), wqkv[...]).astype(BF16)
            whole = []
            for u in range(UNROLL):
                qkv = all_qkv[256 * u : 256 * u + 256]
                parts = []
                for grp in range(3):
                    q, k, v = (qkv[:, C * a + 128 * grp : C * a + 128 * grp + 128] for a in range(3))
                    v = jnp.concatenate([v, ones], 1)
                    att = None
                    for h in range(4):
                        sc = lax.dot_general(q * masks[h], k, (((1,), (1,)), ((), ())), preferred_element_type=F32)
                        sc = sc - jnp.max(sc, axis=-1, keepdims=True)
                        pv = dot(jnp.exp2(sc * expo).astype(BF16), v)
                        pv = pv[:, :128] / pv[:, 128:]
                        att = pv if att is None else jnp.where(heads[h], pv, att)
                    parts.append(att.astype(BF16))
                whole.append(jnp.concatenate(parts, 1))
            second = first + flag * dot(jnp.concatenate(whole, 0), wo[...])
            second = second.astype(BF16).astype(F32)
            for i, part in enumerate(rows):
                put(t, part, second[i * DEV : (i + 1) * DEV])
            return 0

        lax.fori_loop(0, 4 // UNROLL, windows, 0)

        @pl.when(f == 0)
        def _():
            z[0] = take(t, slice(None)).astype(BF16).reshape(DEV, 8, C)

            def send(gg, _):
                spread(z.at[0], o, z_send.at[0], z_recv.at[0], gg)
                return 0

            lax.fori_loop(0, 4, send, 0)
            o[me] = z[0, me]

        @pl.when(f == 1)
        def _():
            def block(p, _):
                parts = [i * 4 + lax.rem(own_g + 2 * p + u, 4) for u in range(2) for i in range(4)]
                second = jnp.concatenate([take(t, pl.ds(part * 64, 64)) for part in parts], 0)
                res = mlp(second, keep[1, 2].astype(F32))
                for i, part in enumerate(parts):
                    z[1, pl.ds(part * WA, WA)] = res[i * 64 : (i + 1) * 64].reshape(8, 8, C)
                for u in range(2):
                    spread(z.at[1], out.at[1], z_send.at[1], z_recv.at[1], 2 * p + u)
                return 0

            lax.fori_loop(0, 2, block, 0)
            pltpu.make_async_copy(z.at[1, me], out.at[1, me], own.at[1]).start()

        return 0

    lax.fori_loop(0, FR, attention, 0)
    arrived(z.at[0], o, z_send.at[0], z_recv.at[0]).wait_recv()

    def home(b, _):
        part = pl.ds(b * 64, 64)
        second = o[part].astype(F32).reshape(512, C)
        r[0, part] = mlp(second, keep[0, 2].astype(F32)).reshape(64, 8, C)
        pltpu.make_async_copy(r.at[0, part], out.at[0, part], own.at[0]).start()
        return 0

    lax.fori_loop(0, 2, home, 0)
    pltpu.make_async_copy(r.at[0], out.at[0], own.at[0]).wait()
    pltpu.make_async_copy(z.at[1, me], out.at[1, me], own.at[1]).wait()
    arrived(z.at[1], out.at[1], z_send.at[1], z_recv.at[1]).wait_recv()
    arrived(z.at[1], out.at[1], z_send.at[1], z_recv.at[1]).wait_send()
    arrived(z.at[0], o, z_send.at[0], z_recv.at[0]).wait_send()
    for f in range(FR):
        arrived(s.at[f], r.at[f], s_send.at[f], s_recv.at[f]).wait_send()


def gather(o, out):
    to = lax.broadcasted_iota(jnp.int32, (CO, CO), 0)
    frm = lax.broadcasted_iota(jnp.int32, (CO, CO), 1)
    order = (frm == 2 * (to % 32) + to // 32).astype(F32).astype(BF16)
    for g in range(o.shape[2]):
        for i in range(4):
            out[0, 4 * g + i] = dot(order, o[0, i, g].reshape(CO, C)).astype(BF16)


def body(frames, keep, we, dwk, bias, wp, wqkv, wo, wi, w2):
    hbm = pl.BlockSpec(memory_space=pl.ANY)
    dma = pltpu.SemaphoreType.DMA
    slots = pltpu.VMEM((FR, DEV, 8, C), BF16)
    arrays = (frames, we, dwk, bias, wp, wqkv, wo, wi, w2)
    result = pl.pallas_call(
        kernel,
        out_shape=jax.ShapeDtypeStruct((FR, DEV, 8, C), BF16),
        in_specs=[hbm, pl.BlockSpec(memory_space=pltpu.SMEM)] + [hbm] * 8,
        out_specs=hbm,
        scratch_shapes=[pltpu.VMEM(a.shape, a.dtype) for a in arrays] + [
            pltpu.VMEM((FR, RO, CO, C), BF16),
            pltpu.VMEM((2, FR, RO, C), BF16),
            pltpu.VMEM((FR, 224, C), BF16),
            pltpu.VMEM((RO + 2, 6, 16, EX), BF16),
            pltpu.VMEM((RO + 2, 6, 16, EX), BF16),
            pltpu.VMEM((10, 16, EX), F32),
            pltpu.VMEM((2, 48, EX), F32),
            pltpu.VMEM((512, EX), BF16),
            slots, slots, slots,
            pltpu.VMEM((DEV, 8, C), BF16),
            pltpu.VMEM((3, DEV * 8, 128), F32),
            pltpu.VMEM((3, 256, 128), F32),
            dma((len(arrays) + 1,)), dma((FR, 8)), dma((FR, 8)),
            dma((FR,)), dma((FR,)), dma((FR,)), dma((FR,)), dma((FR,)),
            pltpu.SemaphoreType.REGULAR,
        ],
        compiler_params=pltpu.CompilerParams(
            collective_id=0, has_side_effects=True, vmem_limit_bytes=60 * 1024 * 1024
        ),
        name="block",
    )(frames, keep, we, dwk, bias, wp, wqkv, wo, wi, w2)
    steps = 1
    return pl.pallas_call(
        gather,
        out_shape=jax.ShapeDtypeStruct(frames.shape, BF16),
        grid=(FR, steps),
        in_specs=[pl.BlockSpec((1, 4, 4 // steps, 8, 8, C), lambda f, g: (f, 0, g, 0, 0, 0))],
        out_specs=pl.BlockSpec((1, RO // steps, CO, C), lambda f, g: (f, g, 0, 0)),
        name="rows",
    )(result.reshape(FR, 4, 4, 8, 8, C))


def solution(mesh):
    in_specs = (P(None, "ha", "wa", None), P(), P(), P(), P(), P(), P(), P(), P(), P())
    return jax.shard_map(body, mesh=mesh, in_specs=in_specs, out_specs=P(None, "ha", "wa", None), check_vma=False)
```

```python
import functools
import math

import jax
import jax.numpy as jnp
from jax import lax
from jax.experimental import pallas as pl
from jax.experimental.pallas import tpu as pltpu
from jax.sharding import PartitionSpec as P

MESH = pl.DeviceIdType.MESH
F32, BF16 = jnp.float32, jnp.bfloat16
HA, WA = 16, 8
DEV = HA * WA
FR, RO, CO, C, EX = 2, 16, 64, 384, 1536
HEADS, HD = 12, 32
UNROLL = 2
CH = 256
GA, GB = math.sqrt(2 / math.pi), math.sqrt(2 / math.pi) * 0.044715


def gelu(v):
    half = 0.5 * v
    return half + half * jnp.tanh(v * (GA + GB * (v * v)))


def gelu_of_half(half):
    return half + half * jnp.tanh(half * (2 * GA + 8 * GB * (half * half)))


def norm(v):
    c = v - jnp.mean(v, axis=-1, keepdims=True)
    return (c * lax.rsqrt(jnp.mean(c * c, axis=-1, keepdims=True) + 1e-05)).astype(BF16)


def put(ref, rows, value):
    for l in range(3):
        ref[l, rows, :] = value[:, 128 * l : 128 * l + 128]


def take(ref, rows):
    return jnp.concatenate([ref[l, rows, :] for l in range(3)], 1)


def dot(a, b):
    return jnp.dot(a, b, preferred_element_type=F32)


def kernel(
    x_hbm, keep, we_hbm, dwk_hbm, bias_hbm, wp_hbm, wqkv_hbm, wo_hbm, wi_hbm, w2_hbm, out,
    x, we, dwk, bias, wp, wqkv, wo, wi, w2,
    xp, cols, hb, e_first, e_second, kb, le, mx, s, r, z, o, t, fs,
    loads, halo_send, halo_recv, s_send, s_recv, z_send, z_recv, own, entry,
):
    ha, wa = lax.axis_index("ha"), lax.axis_index("wa")
    me = ha * WA + wa
    own_x, own_g = ha // 4, lax.rem(ha, 4)
    e = (e_first, e_second)

    def at(h, w):
        return {"ha": h, "wa": w}

    barrier = pltpu.get_barrier_semaphore()
    near = [(ha, lax.rem(wa + i, WA)) for i in range(1, WA)]
    near += [(lax.rem(ha + i, HA), wa) for i in range(1, HA)]
    near += [(lax.rem(ha + i, HA), lax.rem(wa + j, WA)) for i in (1, HA - 1) for j in (1, WA - 1)]
    for h, w in near:
        pl.semaphore_signal(barrier, 1, device_id=at(h, w), device_id_type=MESH)

    arrays = (
        (x_hbm.at[0], x.at[0]), (x_hbm.at[1], x.at[1]), (we_hbm, we), (dwk_hbm, dwk), (bias_hbm, bias), (wp_hbm, wp),
        (wqkv_hbm, wqkv), (wo_hbm, wo), (wi_hbm, wi), (w2_hbm, w2),
    )
    fetch = [pltpu.make_async_copy(src, dst, loads.at[i]) for i, (src, dst) in enumerate(arrays)]
    for c in fetch:
        c.start()

    def permute(f):
        put(t, slice(None), x[f].astype(F32).reshape(RO * CO, C))

        def one(row, _):
            for q in range(4):
                xp[f, row, q * 16 : q * 16 + 16, :] = take(t, pl.ds(row * CO + q, 16, stride=4)).astype(BF16)
            return 0

        lax.fori_loop(0, RO, one, 0)
        for side in range(2):
            cols[side, f] = take(t, pl.ds(side * (CO - 1), RO, stride=CO)).astype(BF16)

    def expand(f, first, count):
        tokens = xp[f, pl.ds(first, count)].reshape(count * 64, C)
        for n in range(0, EX, CH):
            v = gelu(dot(tokens, we[:, n : n + CH]).astype(BF16))
            e[f][pl.ds(first + 1, count), 1:5, :, n : n + CH] = v.reshape(count, 4, 16, CH)

    up, down = lax.rem(ha + HA - 1, HA), lax.rem(ha + 1, HA)
    left, right = lax.rem(wa + WA - 1, WA), lax.rem(wa + 1, WA)

    def halo(f):
        moves = [
            (xp.at[f, RO - 1], hb.at[f, 0:64], (down, wa)),
            (xp.at[f, 0], hb.at[f, 64:128], (up, wa)),
        ]
        for side, w in ((1, right), (0, left)):
            for blk, h in ((0, down), (1, ha), (2, up)):
                first = 128 + (1 - side) * 48 + blk * 16
                moves.append((cols.at[side, f], hb.at[f, first : first + 16], (h, w)))
        return [
            pltpu.make_async_remote_copy(
                src, dst, halo_send.at[f, i], halo_recv.at[f, i], device_id=at(*to), device_id_type=MESH
            )
            for i, (src, dst, to) in enumerate(moves)
        ]

    for f in range(FR):
        fetch[f].wait()
        permute(f)
        if f == 0:
            pl.semaphore_wait(barrier, len(near))
            for h, w in near[: WA - 1]:
                pl.semaphore_signal(entry, 1, device_id=at(h, w), device_id_type=MESH)
        for c in halo(f):
            c.start()
    fetch[2].wait()
    for q in range(2):
        expand(0, q * 8, 8)
    for c in fetch[3:]:
        c.wait()
    for i in range(3):
        for j in range(3):
            kb[3 * i + j] = jnp.broadcast_to(0.5 * dwk[i, j : j + 1, :], (16, EX))
    kb[9] = jnp.broadcast_to(0.5 * bias[...].reshape(1, EX), (16, EX))
    ok_up, ok_down = (ha > 0).astype(F32), (ha < HA - 1).astype(F32)
    ok_side = ((wa > 0).astype(F32), (wa < WA - 1).astype(F32))
    sub = lax.broadcasted_iota(jnp.int32, (16, EX), 0)

    def edges(f):
        tokens = hb[f]
        for n in range(0, EX, CH):
            v = gelu(dot(tokens, we[:, n : n + CH]).astype(BF16))
            e[f][0, 1:5, :, n : n + CH] = (v[0:64] * ok_up.astype(BF16)).reshape(4, 16, CH)
            e[f][RO + 1, 1:5, :, n : n + CH] = (v[64:128] * ok_down.astype(BF16)).reshape(4, 16, CH)
            v = v[128:].astype(F32)
            for side in range(2):
                p = side * 48
                le[side, 0:16, n : n + CH] = v[p : p + 16] * (ok_side[side] * ok_up)
                le[side, 16:32, n : n + CH] = v[p + 16 : p + 32] * ok_side[side]
                le[side, 32:48, n : n + CH] = v[p + 32 : p + 48] * (ok_side[side] * ok_down)

        def fill(p, _):
            for side, (inner, outer, turn, edge) in enumerate(((4, 0, 1, 0), (1, 5, 15, 15))):
                moved = pltpu.roll(e[f][p, inner].astype(F32), turn, 0)
                beyond = jnp.broadcast_to(le[side, pl.ds(15 + p, 1), :], (16, EX))
                e[f][p, outer] = jnp.where(sub == edge, beyond, moved).astype(BF16)
            return 0

        lax.fori_loop(0, RO + 2, fill, 0)


    def partner(i, g, k):
        h, w = lax.rem(own_x + i, 4) * 4 + g, lax.rem(wa + k, WA)
        return h, w

    def spread(src, dst, send, recv, gg):
        g = lax.rem(own_g + gg, 4)
        for i in range(4):
            for k in range(8):
                h, w = partner(i, g, k)
                copy = pltpu.make_async_remote_copy(
                    src.at[h * WA + w], dst.at[me], send, recv, device_id=at(h, w), device_id_type=MESH
                )
                if i + k > 0:
                    copy.start()
                else:
                    pl.when(gg > 0)(copy.start)

    def arrived(src, dst, send, recv):
        return pltpu.make_async_remote_copy(
            src.at[0 : DEV - 1], dst.at[0 : DEV - 1], send, recv, device_id=at(ha, wa), device_id_type=MESH
        )

    pl.semaphore_wait(entry, WA - 1)

    def conv(f):
        flag = keep[f, 0].astype(F32)

        def group(gg, _):
            g = lax.rem(own_g + gg, 4)
            for rr in range(0, 4, 2):
                for n in range(0, EX, 128):
                    taps = [kb[i, :, n : n + 128].astype(BF16)[None] for i in range(10)]
                    for q in range(rr, rr + 2):
                        sums = []
                        for i in range(3):
                            part = [taps[3 * i + j] * e[f][g * 4 + q + i, j : j + 4, :, n : n + 128] for j in range(3)]
                            sums.append(part[0] + part[1] + part[2])
                        acc = (sums[0] + sums[1]) + (sums[2] + taps[9])
                        mx[q * 64 : q * 64 + 64, n : n + 128] = gelu_of_half(acc).reshape(64, 128)
            tokens = xp[f, pl.ds(g * 4, 4)].reshape(256, C)
            put(fs, slice(None), tokens.astype(F32) + flag * dot(mx[0:256], wp[...]))
            for i in range(4):
                for k in range(8):
                    part = take(fs, pl.ds(i * 64 + k, 8, stride=8))
                    s[f, (i * 4 + g) * WA + k] = part.astype(BF16)
            spread(s.at[f], r.at[f], s_send.at[f], s_recv.at[f], gg)
            return 0

        lax.fori_loop(0, 4, group, 0)
        r[f, me] = s[f, me]

    for f in range(FR):
        for c in halo(f):
            c.wait()
        if f == 1:
            for q in range(2):
                expand(1, q * 8, 8)
        edges(f)
        conv(f)

    lane = lax.broadcasted_iota(jnp.int32, (256, 128), 1)
    heads = [(lane >= h * HD) & (lane < (h + 1) * HD) for h in range(4)]
    masks = [m.astype(F32).astype(BF16) for m in heads]
    ones = jnp.ones((256, 128), BF16)
    expo = HD**-0.5 * math.log2(math.e)

    def mlp(second, flag):
        normed = norm(second)
        m = second.shape[0]
        for n in range(0, EX, CH):
            mx[0:m, n : n + CH] = gelu(dot(normed, wi[:, n : n + CH]).astype(BF16))
        return (second + flag * dot(mx[0:m], w2[...])).astype(BF16)

    def attention(f, _):
        arrived(s.at[f], r.at[f], s_send.at[f], s_recv.at[f]).wait_recv()
        put(t, slice(None), r[f].astype(F32).reshape(DEV * 8, C))
        flag = keep[f, 1].astype(F32)

        def windows(p, _):
            rows = [pl.ds(2 * p * UNROLL + i, DEV, stride=8) for i in range(2 * UNROLL)]
            first = jnp.concatenate([take(t, part) for part in rows], 0)
            all_qkv = dot(norm(first), wqkv[...]).astype(BF16)
            whole = []
            for u in range(UNROLL):
                qkv = all_qkv[256 * u : 256 * u + 256]
                parts = []
                for grp in range(3):
                    q, k, v = (qkv[:, C * a + 128 * grp : C * a + 128 * grp + 128] for a in range(3))
                    v = jnp.concatenate([v, ones], 1)
                    att = None
                    for h in range(4):
                        sc = lax.dot_general(q * masks[h], k, (((1,), (1,)), ((), ())), preferred_element_type=F32)
                        sc = sc - jnp.max(sc, axis=-1, keepdims=True)
                        pv = dot(jnp.exp2(sc * expo).astype(BF16), v)
                        pv = pv[:, :128] / pv[:, 128:]
                        att = pv if att is None else jnp.where(heads[h], pv, att)
                    parts.append(att.astype(BF16))
                whole.append(jnp.concatenate(parts, 1))
            second = first + flag * dot(jnp.concatenate(whole, 0), wo[...])
            second = second.astype(BF16).astype(F32)
            for i, part in enumerate(rows):
                put(t, part, second[i * DEV : (i + 1) * DEV])
            return 0

        lax.fori_loop(0, 4 // UNROLL, windows, 0)

        @pl.when(f == 0)
        def _():
            z[0] = take(t, slice(None)).astype(BF16).reshape(DEV, 8, C)

            def send(gg, _):
                spread(z.at[0], o, z_send.at[0], z_recv.at[0], gg)
                return 0

            lax.fori_loop(0, 4, send, 0)
            o[me] = z[0, me]

        @pl.when(f == 1)
        def _():
            def block(p, _):
                parts = [i * 4 + lax.rem(own_g + p, 4) for i in range(4)]
                second = jnp.concatenate([take(t, pl.ds(part * 64, 64)) for part in parts], 0)
                res = mlp(second, keep[1, 2].astype(F32))
                for i, part in enumerate(parts):
                    z[1, pl.ds(part * WA, WA)] = res[i * 64 : (i + 1) * 64].reshape(8, 8, C)
                spread(z.at[1], out.at[1], z_send.at[1], z_recv.at[1], p)
                return 0

            lax.fori_loop(0, 4, block, 0)
            pltpu.make_async_copy(z.at[1, me], out.at[1, me], own.at[1]).start()

        return 0

    lax.fori_loop(0, FR, attention, 0)
    arrived(z.at[0], o, z_send.at[0], z_recv.at[0]).wait_recv()

    def home(b, _):
        part = pl.ds(b * 64, 64)
        second = o[part].astype(F32).reshape(512, C)
        r[0, part] = mlp(second, keep[0, 2].astype(F32)).reshape(64, 8, C)
        pltpu.make_async_copy(r.at[0, part], out.at[0, part], own.at[0]).start()
        return 0

    lax.fori_loop(0, 2, home, 0)
    pltpu.make_async_copy(r.at[0], out.at[0], own.at[0]).wait()
    pltpu.make_async_copy(z.at[1, me], out.at[1, me], own.at[1]).wait()
    arrived(z.at[1], out.at[1], z_send.at[1], z_recv.at[1]).wait_recv()
    arrived(z.at[1], out.at[1], z_send.at[1], z_recv.at[1]).wait_send()
    arrived(z.at[0], o, z_send.at[0], z_recv.at[0]).wait_send()
    for f in range(FR):
        arrived(s.at[f], r.at[f], s_send.at[f], s_recv.at[f]).wait_send()


def gather(o, out):
    to = lax.broadcasted_iota(jnp.int32, (CO, CO), 0)
    frm = lax.broadcasted_iota(jnp.int32, (CO, CO), 1)
    order = (frm == 2 * (to % 32) + to // 32).astype(F32).astype(BF16)
    for g in range(o.shape[2]):
        for i in range(4):
            out[0, 4 * g + i] = dot(order, o[0, i, g].reshape(CO, C)).astype(BF16)


def body(frames, keep, we, dwk, bias, wp, wqkv, wo, wi, w2):
    hbm = pl.BlockSpec(memory_space=pl.ANY)
    dma = pltpu.SemaphoreType.DMA
    slots = pltpu.VMEM((FR, DEV, 8, C), BF16)
    arrays = (frames, we, dwk, bias, wp, wqkv, wo, wi, w2)
    result = pl.pallas_call(
        kernel,
        out_shape=jax.ShapeDtypeStruct((FR, DEV, 8, C), BF16),
        in_specs=[hbm, pl.BlockSpec(memory_space=pltpu.SMEM)] + [hbm] * 8,
        out_specs=hbm,
        scratch_shapes=[pltpu.VMEM(a.shape, a.dtype) for a in arrays] + [
            pltpu.VMEM((FR, RO, CO, C), BF16),
            pltpu.VMEM((2, FR, RO, C), BF16),
            pltpu.VMEM((FR, 224, C), BF16),
            pltpu.VMEM((RO + 2, 6, 16, EX), BF16),
            pltpu.VMEM((RO + 2, 6, 16, EX), BF16),
            pltpu.VMEM((10, 16, EX), F32),
            pltpu.VMEM((2, 48, EX), F32),
            pltpu.VMEM((512, EX), BF16),
            slots, slots, slots,
            pltpu.VMEM((DEV, 8, C), BF16),
            pltpu.VMEM((3, DEV * 8, 128), F32),
            pltpu.VMEM((3, 256, 128), F32),
            dma((len(arrays) + 1,)), dma((FR, 8)), dma((FR, 8)),
            dma((FR,)), dma((FR,)), dma((FR,)), dma((FR,)), dma((FR,)),
            pltpu.SemaphoreType.REGULAR,
        ],
        compiler_params=pltpu.CompilerParams(
            collective_id=0, has_side_effects=True, vmem_limit_bytes=60 * 1024 * 1024
        ),
        name="block",
    )(frames, keep, we, dwk, bias, wp, wqkv, wo, wi, w2)
    steps = 1
    return pl.pallas_call(
        gather,
        out_shape=jax.ShapeDtypeStruct(frames.shape, BF16),
        grid=(FR, steps),
        in_specs=[pl.BlockSpec((1, 4, 4 // steps, 8, 8, C), lambda f, g: (f, 0, g, 0, 0, 0))],
        out_specs=pl.BlockSpec((1, RO // steps, CO, C), lambda f, g: (f, g, 0, 0)),
        name="rows",
    )(result.reshape(FR, 4, 4, 8, 8, C))


def solution(mesh):
    in_specs = (P(None, "ha", "wa", None), P(), P(), P(), P(), P(), P(), P(), P(), P())
    return jax.shard_map(body, mesh=mesh, in_specs=in_specs, out_specs=P(None, "ha", "wa", None), check_vma=False)
```

```python
import functools
import math

import jax
import jax.numpy as jnp
from jax import lax
from jax.experimental import pallas as pl
from jax.experimental.pallas import tpu as pltpu
from jax.sharding import PartitionSpec as P

MESH = pl.DeviceIdType.MESH
F32, BF16 = jnp.float32, jnp.bfloat16
HA, WA = 16, 8
DEV = HA * WA
FR, RO, CO, C, EX = 2, 16, 64, 384, 1536
HEADS, HD = 12, 32
UNROLL = 2
CH = 256
GA, GB = math.sqrt(2 / math.pi), math.sqrt(2 / math.pi) * 0.044715


def gelu(v):
    half = 0.5 * v
    return half + half * jnp.tanh(v * (GA + GB * (v * v)))


def gelu_of_half(half):
    return half + half * jnp.tanh(half * (2 * GA + 8 * GB * (half * half)))


def norm(v):
    c = v - jnp.mean(v, axis=-1, keepdims=True)
    return (c * lax.rsqrt(jnp.mean(c * c, axis=-1, keepdims=True) + 1e-05)).astype(BF16)


def put(ref, rows, value):
    for l in range(3):
        ref[l, rows, :] = value[:, 128 * l : 128 * l + 128]


def take(ref, rows):
    return jnp.concatenate([ref[l, rows, :] for l in range(3)], 1)


def dot(a, b):
    return jnp.dot(a, b, preferred_element_type=F32)


def kernel(
    x_hbm, keep, we_hbm, dwk_hbm, bias_hbm, wp_hbm, wqkv_hbm, wo_hbm, wi_hbm, w2_hbm, out,
    x, we, dwk, bias, wp, wqkv, wo, wi, w2,
    xp, cols, hb, e_first, e_second, kb, le, mx, s, r, z, o, t, fs,
    loads, halo_send, halo_recv, s_send, s_recv, z_send, z_recv, own, entry,
):
    ha, wa = lax.axis_index("ha"), lax.axis_index("wa")
    me = ha * WA + wa
    own_x, own_g = ha // 4, lax.rem(ha, 4)
    e = (e_first, e_second)

    def at(h, w):
        return {"ha": h, "wa": w}

    barrier = pltpu.get_barrier_semaphore()
    near = [(ha, lax.rem(wa + i, WA)) for i in range(1, WA)]
    near += [(lax.rem(ha + i, HA), wa) for i in range(1, HA)]
    near += [(lax.rem(ha + i, HA), lax.rem(wa + j, WA)) for i in (1, HA - 1) for j in (1, WA - 1)]
    for h, w in near:
        pl.semaphore_signal(barrier, 1, device_id=at(h, w), device_id_type=MESH)

    arrays = (
        (x_hbm.at[0], x.at[0]), (x_hbm.at[1], x.at[1]), (we_hbm, we), (dwk_hbm, dwk), (bias_hbm, bias), (wp_hbm, wp),
        (wqkv_hbm, wqkv), (wo_hbm, wo), (wi_hbm, wi), (w2_hbm, w2),
    )
    fetch = [pltpu.make_async_copy(src, dst, loads.at[i]) for i, (src, dst) in enumerate(arrays)]
    for c in fetch:
        c.start()

    def permute(f):
        put(t, slice(None), x[f].astype(F32).reshape(RO * CO, C))

        def one(row, _):
            for q in range(4):
                xp[f, row, q * 16 : q * 16 + 16, :] = take(t, pl.ds(row * CO + q, 16, stride=4)).astype(BF16)
            return 0

        lax.fori_loop(0, RO, one, 0)
        for side in range(2):
            cols[side, f] = take(t, pl.ds(side * (CO - 1), RO, stride=CO)).astype(BF16)

    def expand(f, first, count):
        tokens = xp[f, pl.ds(first, count)].reshape(count * 64, C)
        for n in range(0, EX, CH):
            v = gelu(dot(tokens, we[:, n : n + CH]).astype(BF16))
            e[f][pl.ds(first + 1, count), 1:5, :, n : n + CH] = v.reshape(count, 4, 16, CH)

    up, down = lax.rem(ha + HA - 1, HA), lax.rem(ha + 1, HA)
    left, right = lax.rem(wa + WA - 1, WA), lax.rem(wa + 1, WA)

    def halo(f):
        moves = [
            (xp.at[f, RO - 1], hb.at[f, 0:64], (down, wa)),
            (xp.at[f, 0], hb.at[f, 64:128], (up, wa)),
        ]
        for side, w in ((1, right), (0, left)):
            for blk, h in ((0, down), (1, ha), (2, up)):
                first = 128 + (1 - side) * 48 + blk * 16
                moves.append((cols.at[side, f], hb.at[f, first : first + 16], (h, w)))
        return [
            pltpu.make_async_remote_copy(
                src, dst, halo_send.at[f, i], halo_recv.at[f, i], device_id=at(*to), device_id_type=MESH
            )
            for i, (src, dst, to) in enumerate(moves)
        ]

    for f in range(FR):
        fetch[f].wait()
        permute(f)
        if f == 0:
            pl.semaphore_wait(barrier, len(near))
            for h, w in near[: WA - 1]:
                pl.semaphore_signal(entry, 1, device_id=at(h, w), device_id_type=MESH)
        for c in halo(f):
            c.start()
    fetch[2].wait()
    for q in range(2):
        expand(0, q * 8, 8)
    for c in fetch[3:]:
        c.wait()
    for i in range(3):
        for j in range(3):
            kb[3 * i + j] = jnp.broadcast_to(0.5 * dwk[i, j : j + 1, :], (16, EX))
    kb[9] = jnp.broadcast_to(0.5 * bias[...].reshape(1, EX), (16, EX))
    ok_up, ok_down = (ha > 0).astype(F32), (ha < HA - 1).astype(F32)
    ok_side = ((wa > 0).astype(F32), (wa < WA - 1).astype(F32))
    sub = lax.broadcasted_iota(jnp.int32, (16, EX), 0)

    def edges(f):
        tokens = hb[f]
        for n in range(0, EX, CH):
            v = gelu(dot(tokens, we[:, n : n + CH]).astype(BF16))
            e[f][0, 1:5, :, n : n + CH] = (v[0:64] * ok_up.astype(BF16)).reshape(4, 16, CH)
            e[f][RO + 1, 1:5, :, n : n + CH] = (v[64:128] * ok_down.astype(BF16)).reshape(4, 16, CH)
            v = v[128:].astype(F32)
            for side in range(2):
                p = side * 48
                le[side, 0:16, n : n + CH] = v[p : p + 16] * (ok_side[side] * ok_up)
                le[side, 16:32, n : n + CH] = v[p + 16 : p + 32] * ok_side[side]
                le[side, 32:48, n : n + CH] = v[p + 32 : p + 48] * (ok_side[side] * ok_down)

        def fill(p, _):
            for side, (inner, outer, turn, edge) in enumerate(((4, 0, 1, 0), (1, 5, 15, 15))):
                moved = pltpu.roll(e[f][p, inner].astype(F32), turn, 0)
                beyond = jnp.broadcast_to(le[side, pl.ds(15 + p, 1), :], (16, EX))
                e[f][p, outer] = jnp.where(sub == edge, beyond, moved).astype(BF16)
            return 0

        lax.fori_loop(0, RO + 2, fill, 0)


    def partner(i, g, k):
        h, w = lax.rem(own_x + i, 4) * 4 + g, lax.rem(wa + k, WA)
        return h, w

    def spread(src, dst, send, recv, gg):
        g = lax.rem(own_g + gg, 4)
        for i in range(4):
            for k in range(8):
                h, w = partner(i, g, k)
                copy = pltpu.make_async_remote_copy(
                    src.at[h * WA + w], dst.at[me], send, recv, device_id=at(h, w), device_id_type=MESH
                )
                if i + k > 0:
                    copy.start()
                else:
                    pl.when(gg > 0)(copy.start)

    def arrived(src, dst, send, recv):
        return pltpu.make_async_remote_copy(
            src.at[0 : DEV - 1], dst.at[0 : DEV - 1], send, recv, device_id=at(ha, wa), device_id_type=MESH
        )

    pl.semaphore_wait(entry, WA - 1)

    def conv(f):
        flag = keep[f, 0].astype(F32)

        def group(gg, _):
            g = lax.rem(own_g + gg, 4)
            for rr in range(0, 4, 2):
                for n in range(0, EX, 128):
                    taps = [kb[i, :, n : n + 128].astype(BF16)[None] for i in range(10)]
                    for q in range(rr, rr + 2):
                        sums = []
                        for i in range(3):
                            part = [taps[3 * i + j] * e[f][g * 4 + q + i, j : j + 4, :, n : n + 128] for j in range(3)]
                            sums.append(part[0] + part[1] + part[2])
                        acc = (sums[0] + sums[1]) + (sums[2] + taps[9])
                        mx[q * 64 : q * 64 + 64, n : n + 128] = gelu_of_half(acc).reshape(64, 128)
            tokens = xp[f, pl.ds(g * 4, 4)].reshape(256, C)
            put(fs, slice(None), tokens.astype(F32) + flag * dot(mx[0:256], wp[...]))
            for i in range(4):
                for k in range(8):
                    part = take(fs, pl.ds(i * 64 + k, 8, stride=8))
                    s[f, (i * 4 + g) * WA + k] = part.astype(BF16)
            spread(s.at[f], r.at[f], s_send.at[f], s_recv.at[f], gg)
            return 0

        lax.fori_loop(0, 4, group, 0)
        r[f, me] = s[f, me]

    expand(1, 0, 8)
    for f in range(FR):
        for c in halo(f):
            c.wait()
        if f == 1:
            expand(1, 8, 8)
        edges(f)
        conv(f)

    lane = lax.broadcasted_iota(jnp.int32, (256, 128), 1)
    heads = [(lane >= h * HD) & (lane < (h + 1) * HD) for h in range(4)]
    masks = [m.astype(F32).astype(BF16) for m in heads]
    ones = jnp.ones((256, 128), BF16)
    expo = HD**-0.5 * math.log2(math.e)

    def mlp(second, flag):
        normed = norm(second)
        m = second.shape[0]
        for n in range(0, EX, CH):
            mx[0:m, n : n + CH] = gelu(dot(normed, wi[:, n : n + CH]).astype(BF16))
        return (second + flag * dot(mx[0:m], w2[...])).astype(BF16)

    def attention(f, _):
        arrived(s.at[f], r.at[f], s_send.at[f], s_recv.at[f]).wait_recv()
        put(t, slice(None), r[f].astype(F32).reshape(DEV * 8, C))
        flag = keep[f, 1].astype(F32)

        def windows(p, _):
            rows = [pl.ds(2 * p * UNROLL + i, DEV, stride=8) for i in range(2 * UNROLL)]
            first = jnp.concatenate([take(t, part) for part in rows], 0)
            all_qkv = dot(norm(first), wqkv[...]).astype(BF16)
            whole = []
            for u in range(UNROLL):
                qkv = all_qkv[256 * u : 256 * u + 256]
                parts = []
                for grp in range(3):
                    q, k, v = (qkv[:, C * a + 128 * grp : C * a + 128 * grp + 128] for a in range(3))
                    v = jnp.concatenate([v, ones], 1)
                    att = None
                    for h in range(4):
                        sc = lax.dot_general(q * masks[h], k, (((1,), (1,)), ((), ())), preferred_element_type=F32)
                        sc = sc - jnp.max(sc, axis=-1, keepdims=True)
                        pv = dot(jnp.exp2(sc * expo).astype(BF16), v)
                        pv = pv[:, :128] / pv[:, 128:]
                        att = pv if att is None else jnp.where(heads[h], pv, att)
                    parts.append(att.astype(BF16))
                whole.append(jnp.concatenate(parts, 1))
            second = first + flag * dot(jnp.concatenate(whole, 0), wo[...])
            second = second.astype(BF16).astype(F32)
            for i, part in enumerate(rows):
                put(t, part, second[i * DEV : (i + 1) * DEV])
            return 0

        lax.fori_loop(0, 4 // UNROLL, windows, 0)

        @pl.when(f == 0)
        def _():
            z[0] = take(t, slice(None)).astype(BF16).reshape(DEV, 8, C)

            def send(gg, _):
                spread(z.at[0], o, z_send.at[0], z_recv.at[0], gg)
                return 0

            lax.fori_loop(0, 4, send, 0)
            o[me] = z[0, me]

        @pl.when(f == 1)
        def _():
            def block(p, _):
                parts = [i * 4 + lax.rem(own_g + p, 4) for i in range(4)]
                second = jnp.concatenate([take(t, pl.ds(part * 64, 64)) for part in parts], 0)
                res = mlp(second, keep[1, 2].astype(F32))
                for i, part in enumerate(parts):
                    z[1, pl.ds(part * WA, WA)] = res[i * 64 : (i + 1) * 64].reshape(8, 8, C)
                spread(z.at[1], out.at[1], z_send.at[1], z_recv.at[1], p)
                return 0

            lax.fori_loop(0, 4, block, 0)
            pltpu.make_async_copy(z.at[1, me], out.at[1, me], own.at[1]).start()

        return 0

    lax.fori_loop(0, FR, attention, 0)
    arrived(z.at[0], o, z_send.at[0], z_recv.at[0]).wait_recv()

    def home(b, _):
        part = pl.ds(b * 64, 64)
        second = o[part].astype(F32).reshape(512, C)
        r[0, part] = mlp(second, keep[0, 2].astype(F32)).reshape(64, 8, C)
        pltpu.make_async_copy(r.at[0, part], out.at[0, part], own.at[0]).start()
        return 0

    lax.fori_loop(0, 2, home, 0)
    pltpu.make_async_copy(r.at[0], out.at[0], own.at[0]).wait()
    pltpu.make_async_copy(z.at[1, me], out.at[1, me], own.at[1]).wait()
    arrived(z.at[1], out.at[1], z_send.at[1], z_recv.at[1]).wait_recv()
    arrived(z.at[1], out.at[1], z_send.at[1], z_recv.at[1]).wait_send()
    arrived(z.at[0], o, z_send.at[0], z_recv.at[0]).wait_send()
    for f in range(FR):
        arrived(s.at[f], r.at[f], s_send.at[f], s_recv.at[f]).wait_send()


def gather(o, out):
    to = lax.broadcasted_iota(jnp.int32, (CO, CO), 0)
    frm = lax.broadcasted_iota(jnp.int32, (CO, CO), 1)
    order = (frm == 2 * (to % 32) + to // 32).astype(F32).astype(BF16)
    for g in range(o.shape[2]):
        for i in range(4):
            out[0, 4 * g + i] = dot(order, o[0, i, g].reshape(CO, C)).astype(BF16)


def body(frames, keep, we, dwk, bias, wp, wqkv, wo, wi, w2):
    hbm = pl.BlockSpec(memory_space=pl.ANY)
    dma = pltpu.SemaphoreType.DMA
    slots = pltpu.VMEM((FR, DEV, 8, C), BF16)
    arrays = (frames, we, dwk, bias, wp, wqkv, wo, wi, w2)
    result = pl.pallas_call(
        kernel,
        out_shape=jax.ShapeDtypeStruct((FR, DEV, 8, C), BF16),
        in_specs=[hbm, pl.BlockSpec(memory_space=pltpu.SMEM)] + [hbm] * 8,
        out_specs=hbm,
        scratch_shapes=[pltpu.VMEM(a.shape, a.dtype) for a in arrays] + [
            pltpu.VMEM((FR, RO, CO, C), BF16),
            pltpu.VMEM((2, FR, RO, C), BF16),
            pltpu.VMEM((FR, 224, C), BF16),
            pltpu.VMEM((RO + 2, 6, 16, EX), BF16),
            pltpu.VMEM((RO + 2, 6, 16, EX), BF16),
            pltpu.VMEM((10, 16, EX), F32),
            pltpu.VMEM((2, 48, EX), F32),
            pltpu.VMEM((512, EX), BF16),
            slots, slots, slots,
            pltpu.VMEM((DEV, 8, C), BF16),
            pltpu.VMEM((3, DEV * 8, 128), F32),
            pltpu.VMEM((3, 256, 128), F32),
            dma((len(arrays) + 1,)), dma((FR, 8)), dma((FR, 8)),
            dma((FR,)), dma((FR,)), dma((FR,)), dma((FR,)), dma((FR,)),
            pltpu.SemaphoreType.REGULAR,
        ],
        compiler_params=pltpu.CompilerParams(
            collective_id=0, has_side_effects=True, vmem_limit_bytes=60 * 1024 * 1024
        ),
        name="block",
    )(frames, keep, we, dwk, bias, wp, wqkv, wo, wi, w2)
    steps = 1
    return pl.pallas_call(
        gather,
        out_shape=jax.ShapeDtypeStruct(frames.shape, BF16),
        grid=(FR, steps),
        in_specs=[pl.BlockSpec((1, 4, 4 // steps, 8, 8, C), lambda f, g: (f, 0, g, 0, 0, 0))],
        out_specs=pl.BlockSpec((1, RO // steps, CO, C), lambda f, g: (f, g, 0, 0)),
        name="rows",
    )(result.reshape(FR, 4, 4, 8, 8, C))


def solution(mesh):
    in_specs = (P(None, "ha", "wa", None), P(), P(), P(), P(), P(), P(), P(), P(), P())
    return jax.shard_map(body, mesh=mesh, in_specs=in_specs, out_specs=P(None, "ha", "wa", None), check_vma=False)
```
